256 devices in a mesh: depth: 4 (over x), scan: 64 (over z, y, core).
Axes of the slice: x: 4, y: 4, z: 8, core: 2. Of those that a mesh axis runs over, the one named last changes fastest.
Arguments:
- transmission: float32 [4, 2, 8192, 1024], P('depth', None, 'scan'), may hold values from 0.4 to 1
- probe_wave: float32 [2, 256, 256], replicated, may hold values from -5 to 5
- prop_phase: float32 [256, 256], replicated, may hold values from -3.140625 to 3.140625
- measured: float32 [256, 256, 256], P('scan'), may hold values from 0.2 to 2
- scan_rows: int32 [256], P('scan'), may hold values from 0 to 127
- scan_cols: int32 [256], P('scan'), may hold values from 0 to 768
- live_counts: int32 [64], P('scan'), may hold values from 1 to 4, 160 in all
Outputs:
- object_grad: float32 [4, 2, 8192, 1024], P('depth', None, 'scan')
The draws below stay inside these ranges and needn't reach their ends.
Inputs may be any that keep to these rules, and one draw needn't show every extreme that they name: `live_counts`: the largest count equals 4.
All inputs are finite; a program needn't handle non-finite values. No bound on the sum of `live_counts` on one device may be relied on, other than what follows from the above.
Results may differ from the reference program's by a relative error of at most 0.035.
Values may be sent and summed in bfloat16 or wider, within the bound.
A program may use at most 64 MiB of HBM per device.

```python
import math
import jax
import jax.numpy as jnp
import numpy as np
from jax import lax

W = 256
P_DEV = 4
TILE = 128
OCOLS = 1024
SLICES = 4
PROBES = 256
NROWS = 8192
N_SCAN = 64


def with_ends(drawn, own_key, smallest, high):
    extent = drawn.shape
    index_at = [jax.random.randint(jax.random.fold_in(own_key, axis), (), 0, extent[axis]) for axis in range(len(extent))]
    drawn = drawn.at[tuple(index_at)].set(smallest)
    longest = extent.index(max(extent))
    index_at[longest] = (index_at[longest] + 1) % extent[longest]
    return drawn.at[tuple(index_at)].set(high)


def block_levels(rng, extent, pieces, smallest, largest):
    gain = 1.0
    for axis_at, shards_of in pieces:
        steps = jax.random.uniform(jax.random.fold_in(jax.random.fold_in(rng, 6), axis_at), (shards_of,), jnp.float32, smallest / len(pieces), largest / len(pieces))
        gain = gain * jnp.repeat(jnp.exp(steps), extent[axis_at] // shards_of).reshape((-1,) + (1,) * (len(extent) - 1 - axis_at))
    return gain


def profile(count, total, bound, lean):
    portions = [(1 << 20) // math.isqrt(grade ** lean) + 1 for grade in range(2, count + 1)]
    rest, counts = total - bound - (count - 1), [1] * (count - 1)
    while rest > 0:
        candidates = [i for i in range(count - 1) if counts[i] < bound]
        whole, budget = sum([portions[i] for i in candidates]), rest
        for i in candidates:
            addition = min(bound - counts[i], max(1, budget * portions[i] // whole), rest)
            counts[i] = counts[i] + addition
            rest = rest - addition
    return np.array([bound] + counts)


def ragged_sizes(own_key, count, total, limit, slope):
    if count == 2:
        one = jax.random.randint(own_key, (), max(1, total - limit), min(limit, total - 1) + 1)
        return jnp.stack([one, total - one])
    lengths = jnp.asarray(profile(count, total, limit, slope), jnp.int32)
    pairs = (count - 1) // 2
    source_of, sink = lengths[1:1 + 2 * pairs:2], lengths[2:2 + 2 * pairs:2]
    slack = jnp.minimum(source_of - 1, limit - sink)
    passed = jax.random.randint(jax.random.fold_in(own_key, 1), (pairs,), 0, 1 << 20) % (slack + 1)
    lengths = lengths.at[1:1 + 2 * pairs:2].set(source_of - passed).at[2:2 + 2 * pairs:2].set(sink + passed)
    return lengths[jax.random.permutation(jax.random.fold_in(own_key, 2), count)]


def gaussian(rng, dims, spread, limit, kind=jnp.bfloat16):
    return jnp.clip(spread * jax.random.normal(rng, dims, jnp.float32), -limit, limit).astype(kind)


def setup_inputs(seed: int = 0) -> dict:
    arg_keys = jax.random.split(jax.random.key(seed), 8)
    transmission = jnp.clip(0.4 + 0.6 * jax.random.uniform(arg_keys[0], (SLICES, 2, NROWS, OCOLS), jnp.float32) ** block_levels(arg_keys[0], (SLICES, 2, NROWS, OCOLS), ((0, 4), (2, 64)), -0.2, 0.2), 0.4, 1.0)
    probe_wave = gaussian(arg_keys[1], (2, W, W), 0.7, 5.0, jnp.float32)
    prop_phase = jnp.clip(jax.random.uniform(arg_keys[2], (W, W), jnp.float32, -3.140625, 3.140625), -3.140625, 3.140625)
    measured = jnp.clip(0.2 + 1.8 * jax.random.uniform(arg_keys[3], (PROBES, W, W), jnp.float32) ** block_levels(arg_keys[3], (PROBES, W, W), ((0, 64),), -0.2, 0.2), 0.2, 2.0)
    scan_rows = with_ends(jax.random.randint(arg_keys[4], (PROBES,), 0, TILE), jax.random.fold_in(arg_keys[4], 1), 0, TILE - 1).astype(jnp.int32)
    scan_cols = with_ends(jax.random.randint(arg_keys[5], (PROBES,), 0, OCOLS - W + 1), jax.random.fold_in(arg_keys[5], 1), 0, OCOLS - W).astype(jnp.int32)
    live_counts = ragged_sizes(arg_keys[6], N_SCAN, N_SCAN * P_DEV * 5 // 8, P_DEV, 2).astype(jnp.int32)
    return {"transmission": transmission, "probe_wave": probe_wave, "prop_phase": prop_phase, "measured": measured, "scan_rows": scan_rows, "scan_cols": scan_cols, "live_counts": live_counts}


epsilon = 1.0

def dft_tables(pixels):
    indices = jnp.arange(pixels, dtype=jnp.int32)
    product = indices[:, None] * indices[None, :] % pixels
    angles = product.astype(jnp.float32) * (2.0 * math.pi / pixels)
    norm_scale = 1.0 / math.sqrt(pixels)
    return ((jnp.cos(angles) * norm_scale).astype(jnp.bfloat16), (-jnp.sin(angles) * norm_scale).astype(jnp.bfloat16))

def transform2d(values, table_re, table_im):
    hp = lax.Precision.HIGHEST
    vals = values.astype(jnp.float32)
    left_re = jnp.einsum('jk,bckl->bcjl', table_re.astype(jnp.float32), vals, precision=hp)
    left_im = jnp.einsum('jk,bckl->bcjl', table_im.astype(jnp.float32), vals, precision=hp)
    inner = jnp.stack([left_re[:, 0] - left_im[:, 1], left_re[:, 1] + left_im[:, 0]], axis=1).astype(jnp.bfloat16)
    inner = inner.astype(jnp.float32)
    right_re = jnp.einsum('bcjk,kl->bcjl', inner, table_re.astype(jnp.float32), precision=hp)
    right_im = jnp.einsum('bcjk,kl->bcjl', inner, table_im.astype(jnp.float32), precision=hp)
    return (right_re[:, 0] - right_im[:, 1], right_re[:, 1] + right_im[:, 0])

def advance(wave, patch, table_re, table_im, prop_re, prop_im):
    wave32 = wave.astype(jnp.float32)
    chi = jnp.stack([patch[:, 0] * wave32[:, 0] - patch[:, 1] * wave32[:, 1], patch[:, 0] * wave32[:, 1] + patch[:, 1] * wave32[:, 0]], axis=1).astype(jnp.bfloat16)
    spec_re, spec_im = transform2d(chi, table_re, table_im)
    turned = jnp.stack([spec_re * prop_re - spec_im * prop_im, spec_re * prop_im + spec_im * prop_re], axis=1).astype(jnp.bfloat16)
    out_re, out_im = transform2d(turned, table_re, -table_im)
    return jnp.stack([out_re, out_im], axis=1).astype(jnp.bfloat16)

def retreat(adjoint, patch, incident, table_re, table_im, prop_re, prop_im):
    back_re, back_im = transform2d(adjoint, table_re, table_im)
    turned = jnp.stack([back_re * prop_re + back_im * prop_im, back_im * prop_re - back_re * prop_im], axis=1).astype(jnp.bfloat16)
    mu_re, mu_im = transform2d(turned, table_re, -table_im)
    inc = incident.astype(jnp.float32)
    contrib = jnp.stack([inc[:, 0] * mu_re + inc[:, 1] * mu_im, inc[:, 0] * mu_im - inc[:, 1] * mu_re], axis=1)
    onward = jnp.stack([patch[:, 0] * mu_re + patch[:, 1] * mu_im, patch[:, 0] * mu_im - patch[:, 1] * mu_re], axis=1).astype(jnp.bfloat16)
    return (contrib, onward)

def detector(leaving, measured, live_mask, table_re, table_im):
    far_re, far_im = transform2d(leaving, table_re, table_im)
    modulus = jnp.sqrt(far_re * far_re + far_im * far_im + epsilon)
    factor = live_mask[:, None, None] * (1.0 - measured / modulus)
    resid = jnp.stack([factor * far_re, factor * far_im], axis=1).astype(jnp.bfloat16)
    start_re, start_im = transform2d(resid, table_re, -table_im)
    return jnp.stack([start_re, start_im], axis=1).astype(jnp.bfloat16)

def reference(transmission, probe_wave, prop_phase, measured, scan_rows, scan_cols, live_counts):
    pixels = probe_wave.shape[-1]
    slices_all = transmission.shape[0]
    nrows_all = transmission.shape[2]
    table_re, table_im = dft_tables(pixels)
    prop_re = jnp.cos(prop_phase)
    prop_im = jnp.sin(prop_phase)
    extended = jnp.concatenate([transmission, transmission[:, :, :pixels]], axis=2)
    probe_b = probe_wave.astype(jnp.bfloat16)[None]
    slot_ids = jnp.arange(PROBES, dtype=jnp.int32)
    tile_ids = slot_ids // P_DEV
    live_mask = (slot_ids - tile_ids * P_DEV < live_counts[tile_ids]).astype(jnp.float32)
    row_base = (tile_ids * TILE + scan_rows).astype(jnp.int32)
    zero_idx = jnp.zeros((), jnp.int32)

    def one_probe(gradient, probe_item):
        row_start, col_start, amplitude, live_flag = probe_item
        wave = probe_b
        patches = []
        incidents = []
        for slice_no in range(slices_all):
            patch = lax.dynamic_slice(extended[slice_no], (zero_idx, row_start, col_start), (2, pixels, pixels))[None]
            patches.append(patch)
            incidents.append(wave)
            wave = advance(wave, patch, table_re, table_im, prop_re, prop_im)
        adjoint = detector(wave, amplitude[None], live_flag[None], table_re, table_im)
        for slice_no in range(slices_all - 1, -1, -1):
            contrib, adjoint = retreat(adjoint, patches[slice_no], incidents[slice_no], table_re, table_im, prop_re, prop_im)
            where_at = (jnp.asarray(slice_no, jnp.int32), zero_idx, row_start, col_start)
            current = lax.dynamic_slice(gradient, where_at, (1, 2, pixels, pixels))
            gradient = lax.dynamic_update_slice(gradient, current + contrib, where_at)
        return (gradient, None)
    start_grad = jnp.zeros((slices_all, 2, nrows_all + pixels, transmission.shape[3]), jnp.float32)
    gradient, _ = lax.scan(one_probe, start_grad, (row_base, scan_cols, measured, live_mask))
    folded = gradient[:, :, :nrows_all]
    overflow = gradient[:, :, nrows_all:]
    return folded.at[:, :, :pixels].add(overflow)
```

```python
import functools
import math

import jax
import jax.numpy as jnp
import numpy as np
from jax import lax
from jax.experimental import pallas as pl
from jax.experimental.pallas import tpu as pltpu
from jax.sharding import PartitionSpec as P

MESH = pl.DeviceIdType.MESH
BF16 = jnp.bfloat16
F32 = jnp.float32


def dft_blocks(pixels):
    index = np.arange(pixels)
    angles = (index[:, None] * index[None, :] % pixels) * (2.0 * math.pi / pixels)
    scale = 1.0 / math.sqrt(pixels)
    re, im = np.cos(angles) * scale, -np.sin(angles) * scale
    first = np.block([[re, -im], [im, re]])
    return jnp.asarray(first, F32).astype(BF16), jnp.asarray(first.T, F32).astype(BF16)


def kernel(
    tile_hbm, probe_hbm, phase_hbm, meas_hbm, rows_s, cols_s, live_s, t1_hbm, t2_hbm,
    out_ref,
    tile32, tile16, probe32, phase, meas, t1, t2, par_out, par_in,
    lower, upper, crops_b, crops_a, patch, prop, psi, xs, us, grads, came,
    strip_low, strip_high, got_low, got_high,
    load_sem, par_sem, tile_sem_s, tile_sem_r, meas_sem,
    bx_s, bx_r, ax_s, ax_r, gb_s, gb_r, ga_s, ga_r, strip_s, strip_r,
):
    depth = lax.axis_index("depth")
    scan = lax.axis_index("scan")
    n_depth = lax.axis_size("depth")
    n_scan = lax.axis_size("scan")
    after = lax.rem(scan + 1, n_scan)
    before = lax.rem(scan + n_scan - 1, n_scan)
    half, width = patch.shape[3], patch.shape[4]
    blocks = tile32.shape[2] // width
    slots = n_depth

    def peer(offset):
        return (lax.rem(depth + offset, n_depth), scan)

    loads = [
        pltpu.make_async_copy(tile_hbm.at[0, 0], tile32.at[0], load_sem.at[0]),
        pltpu.make_async_copy(tile_hbm.at[0, 1], tile32.at[1], load_sem.at[1]),
        pltpu.make_async_copy(probe_hbm, probe32, load_sem.at[2]),
        pltpu.make_async_copy(phase_hbm, phase, load_sem.at[3]),
        pltpu.make_async_copy(t1_hbm, t1, load_sem.at[4]),
        pltpu.make_async_copy(t2_hbm, t2, load_sem.at[5]),
    ]
    for load in loads:
        load.start()

    barrier = pltpu.get_barrier_semaphore()
    for offset in range(1, n_depth):
        pl.semaphore_signal(barrier, inc=1, device_id=peer(offset), device_id_type=MESH)
    pl.semaphore_signal(barrier, inc=1, device_id=(depth, after), device_id_type=MESH)
    pl.semaphore_signal(barrier, inc=1, device_id=(depth, before), device_id_type=MESH)
    for slot in range(slots):
        par_out[slot : slot + 1, :] = jnp.full((1, width), rows_s[slot], jnp.int32)
        par_out[slots + slot : slots + slot + 1, :] = jnp.full((1, width), cols_s[slot], jnp.int32)
    par_out[2 * slots : 2 * slots + 1, :] = jnp.full((1, width), live_s[0], jnp.int32)
    pl.semaphore_wait(barrier, n_depth + 1)

    def send(src, dst, s_sem, r_sem, device):
        return pltpu.make_async_remote_copy(
            src_ref=src, dst_ref=dst, send_sem=s_sem, recv_sem=r_sem,
            device_id=device, device_id_type=MESH,
        )

    par_copy = send(par_out, par_in, par_sem.at[0], par_sem.at[1], (depth, after))
    par_copy.start()
    tile_copies = []
    for plane in range(2):
        loads[plane].wait()
        tile16[plane] = tile32[plane].astype(BF16)
        pair = [
            send(tile16.at[plane], lower.at[plane], tile_sem_s.at[0, plane],
                 tile_sem_r.at[0, plane], (depth, after)),
            send(tile16.at[plane], upper.at[plane], tile_sem_s.at[1, plane],
                 tile_sem_r.at[1, plane], (depth, before)),
        ]
        for copy in pair:
            copy.start()
        tile_copies.append(pair)
    meas_copy = send(meas_hbm.at[depth], meas, meas_sem.at[0], meas_sem.at[1], (depth, after))
    meas_copy.start()

    row_at = lax.broadcasted_iota(jnp.int32, (half, width), 0)
    lane_at = lax.broadcasted_iota(jnp.int32, (half, width), 1)

    def block_of(slot):
        first = jnp.broadcast_to(par_in[pl.ds(slots + slot, 1), :], (half, width))
        return (first >> 8) + jnp.where(lane_at < (first & (width - 1)), 1, 0)

    def from_low(slot):
        return row_at >= jnp.broadcast_to(par_in[pl.ds(slot, 1), :], (half, width))

    par_copy.wait_recv()
    b_copies = []
    for offset in range(n_depth):
        block = block_of(lax.rem(depth + offset, n_depth))
        for plane in range(2):
            piece = tile32[plane, :, :width]
            for at in range(1, blocks):
                piece = jnp.where(block == at, tile32[plane, :, at * width : (at + 1) * width], piece)
            if offset == 0:
                patch[depth, 1, plane] = piece.astype(BF16)
            else:
                crops_b[offset - 1, plane] = piece.astype(BF16)
        if offset:
            copy = send(crops_b.at[offset - 1], patch.at[depth, 1], bx_s.at[offset - 1],
                        bx_r.at[offset - 1], peer(offset))
            copy.start()
            b_copies.append(copy)

    loads[2].wait()
    loads[3].wait()
    big_row = lax.broadcasted_iota(jnp.int32, (width, width), 0)
    big_lane = lax.broadcasted_iota(jnp.int32, (width, width), 1)
    own_row = jnp.broadcast_to(par_in[pl.ds(depth, 1), :], (width, width))
    own_col = jnp.broadcast_to(par_in[pl.ds(slots + depth, 1), :], (width, width))
    down = jnp.where(((big_row - own_row) & (width - 1)) == big_lane, 1.0, 0.0).astype(BF16)
    across = jnp.where(((big_row + own_col) & (width - 1)) == big_lane, 1.0, 0.0).astype(BF16)
    for plane in range(2):
        rolled = jnp.dot(down, probe32[plane].astype(BF16), preferred_element_type=F32)
        rolled = jnp.dot(rolled.astype(BF16), across, preferred_element_type=F32)
        psi[0, plane] = rolled.astype(BF16)
    prop[0] = jnp.cos(phase[...])
    prop[1] = jnp.sin(phase[...])

    a_copies = []
    for plane in range(2):
        for copy in tile_copies[plane]:
            copy.wait_recv()
        for offset in range(n_depth):
            slot = lax.rem(depth + offset, n_depth)
            block, low = block_of(slot), from_low(slot)
            piece = jnp.zeros((half, width), F32)
            for at in range(blocks):
                span = slice(at * width, (at + 1) * width)
                merged = jnp.where(
                    low, lower[plane, :, span].astype(F32), upper[plane, :, span].astype(F32)
                )
                piece = jnp.where(block == at, merged, piece)
            if offset == 0:
                patch[depth, 0, plane] = piece.astype(BF16)
            else:
                crops_a[offset - 1, plane] = piece.astype(BF16)
                copy = send(crops_a.at[offset - 1, plane], patch.at[depth, 0, plane],
                            ax_s.at[offset - 1, plane], ax_r.at[offset - 1, plane],
                            peer(offset))
                copy.start()
                a_copies.append(copy)

    loads[4].wait()
    loads[5].wait()

    def transform(left, right):
        inner = jnp.dot(left[...], xs[...], preferred_element_type=F32)
        us[:, :width] = inner[:width].astype(BF16)
        us[:, width:] = inner[width:].astype(BF16)
        both = jnp.dot(us[...], right[...], preferred_element_type=F32)
        return both[:, :width], both[:, width:]

    def keep(re, im):
        xs[:width] = re.astype(BF16)
        xs[width:] = im.astype(BF16)

    def forward(at, carry):
        @pl.when(at != depth)
        def _():
            offset = lax.rem(depth + n_depth - at, n_depth) - 1
            send(crops_b.at[offset], patch.at[at, 1], bx_s.at[offset], bx_r.at[offset],
                 (at, scan)).wait_recv()
            for plane in range(2):
                send(crops_a.at[offset, plane], patch.at[at, 0, plane], ax_s.at[offset, plane],
                     ax_r.at[offset, plane], (at, scan)).wait_recv()

        for part in range(2):
            span = slice(part * half, (part + 1) * half)
            tr, ti = patch[at, part, 0].astype(F32), patch[at, part, 1].astype(F32)
            pr, pi = psi[at, 0, span].astype(F32), psi[at, 1, span].astype(F32)
            xs[part * half : (part + 1) * half] = (tr * pr - ti * pi).astype(BF16)
            xs[width + part * half : width + (part + 1) * half] = (tr * pi + ti * pr).astype(BF16)
        re, im = transform(t1, t2)
        keep(re * prop[0] - im * prop[1], re * prop[1] + im * prop[0])
        re, im = transform(t2, t1)
        psi[at + 1, 0] = re.astype(BF16)
        psi[at + 1, 1] = im.astype(BF16)
        return carry

    lax.fori_loop(0, n_depth, forward, 0)

    xs[:width] = psi[n_depth, 0]
    xs[width:] = psi[n_depth, 1]
    re, im = transform(t1, t2)
    meas_copy.wait_recv()
    live = jnp.where(jnp.broadcast_to(par_in[2 * slots : 2 * slots + 1, :], (width, width)) > depth, 1.0, 0.0)
    factor = live * (1.0 - meas[...] / jnp.sqrt(re * re + im * im + 1.0))
    keep(factor * re, factor * im)
    re, im = transform(t2, t1)
    keep(re, im)

    def grad_copies(at):
        offset = lax.rem(at + n_depth - depth, n_depth) - 1
        device = (at, scan)
        found = [
            send(grads.at[at, 0, plane], came.at[depth, 0, plane], ga_s.at[offset, plane],
                 ga_r.at[offset, plane], device)
            for plane in range(2)
        ]
        found.append(
            send(grads.at[at, 1], came.at[depth, 1], gb_s.at[offset], gb_r.at[offset], device)
        )
        return found

    def backward(step, carry):
        at = n_depth - 1 - step
        re, im = transform(t1, t2)
        keep(re * prop[0] + im * prop[1], im * prop[0] - re * prop[1])
        mu_re, mu_im = transform(t2, t1)
        for part in range(2):
            span = slice(part * half, (part + 1) * half)
            re, im = mu_re[span], mu_im[span]
            tr, ti = patch[at, part, 0].astype(F32), patch[at, part, 1].astype(F32)
            pr, pi = psi[at, 0, span].astype(F32), psi[at, 1, span].astype(F32)
            grads[at, part, 0] = (pr * re + pi * im).astype(BF16)
            grads[at, part, 1] = (pr * im - pi * re).astype(BF16)
            xs[part * half : (part + 1) * half] = (tr * re + ti * im).astype(BF16)
            xs[width + part * half : width + (part + 1) * half] = (tr * im - ti * re).astype(BF16)

        @pl.when(at != depth)
        def _():
            for copy in grad_copies(at):
                copy.start()

        return carry

    lax.fori_loop(0, n_depth, backward, 0)

    def arrived(offset, part, plane):
        return send(grads.at[0, part, plane], came.at[0, part, plane], ga_s.at[offset, plane],
                    ga_r.at[offset, plane], (depth, scan))

    for part in range(2):
        for plane in range(2):
            came[depth, part, plane] = grads[depth, part, plane]
    strip_copies = []
    for plane in range(2):
        for offset in range(n_depth - 1):
            arrived(offset, 0, plane).wait_recv()
        for at in range(blocks):
            low_sum = jnp.zeros((half, width), F32)
            high_sum = jnp.zeros((half, width), F32)
            for slot in range(slots):
                value = jnp.where(block_of(slot) == at, came[slot, 0, plane].astype(F32), 0.0)
                kept = jnp.where(from_low(slot), value, 0.0)
                low_sum = low_sum + kept
                high_sum = high_sum + (value - kept)
            span = slice(at * width, (at + 1) * width)
            strip_low[plane, :, span] = low_sum.astype(BF16)
            strip_high[plane, :, span] = high_sum.astype(BF16)
        pair = [
            send(strip_low.at[plane], got_low.at[plane], strip_s.at[0, plane],
                 strip_r.at[0, plane], (depth, before)),
            send(strip_high.at[plane], got_high.at[plane], strip_s.at[1, plane],
                 strip_r.at[1, plane], (depth, after)),
        ]
        for copy in pair:
            copy.start()
        strip_copies.append(pair)

    for offset in range(n_depth - 1):
        send(grads.at[0, 1], came.at[0, 1], gb_s.at[offset], gb_r.at[offset],
             (depth, scan)).wait_recv()
    for plane in range(2):
        for at in range(blocks):
            total = jnp.zeros((half, width), F32)
            for slot in range(slots):
                total = total + jnp.where(block_of(slot) == at, came[slot, 1, plane].astype(F32), 0.0)
            tile32[plane, :, at * width : (at + 1) * width] = total
    for plane in range(2):
        for copy in strip_copies[plane]:
            copy.wait_recv()
        out_ref[0, plane] = (
            tile32[plane] + got_low[plane].astype(F32) + got_high[plane].astype(F32)
        )

    par_copy.wait_send()
    meas_copy.wait_send()
    for copy in b_copies + a_copies:
        copy.wait_send()
    for pair in tile_copies + strip_copies:
        for copy in pair:
            copy.wait_send()
    for step in range(1, n_depth):
        for copy in grad_copies(lax.rem(depth + step, n_depth)):
            copy.wait_send()


def body(transmission, probe_wave, prop_phase, measured, scan_rows, scan_cols, live_counts):
    width = probe_wave.shape[-1]
    half = transmission.shape[2]
    columns = transmission.shape[3]
    n_depth = lax.axis_size("depth")
    t1, t2 = dft_blocks(width)
    dma = pltpu.SemaphoreType.DMA
    others = n_depth - 1
    scratch = [
        pltpu.VMEM((2, half, columns), F32),
        pltpu.VMEM((2, half, columns), BF16),
        pltpu.VMEM((2, width, width), F32),
        pltpu.VMEM((width, width), F32),
        pltpu.VMEM((width, width), F32),
        pltpu.VMEM((2 * width, 2 * width), BF16),
        pltpu.VMEM((2 * width, 2 * width), BF16),
        pltpu.VMEM((16, width), jnp.int32),
        pltpu.VMEM((16, width), jnp.int32),
        pltpu.VMEM((2, half, columns), BF16),
        pltpu.VMEM((2, half, columns), BF16),
        pltpu.VMEM((others, 2, half, width), BF16),
        pltpu.VMEM((others, 2, half, width), BF16),
        pltpu.VMEM((n_depth, 2, 2, half, width), BF16),
        pltpu.VMEM((2, width, width), F32),
        pltpu.VMEM((n_depth + 1, 2, width, width), BF16),
        pltpu.VMEM((2 * width, width), BF16),
        pltpu.VMEM((width, 2 * width), BF16),
        pltpu.VMEM((n_depth, 2, 2, half, width), BF16),
        pltpu.VMEM((n_depth, 2, 2, half, width), BF16),
        pltpu.VMEM((2, half, columns), BF16),
        pltpu.VMEM((2, half, columns), BF16),
        pltpu.VMEM((2, half, columns), BF16),
        pltpu.VMEM((2, half, columns), BF16),
        dma((6,)),
        dma((2,)),
        dma((2, 2)),
        dma((2, 2)),
        dma((2,)),
        dma((others,)),
        dma((others,)),
        dma((others, 2)),
        dma((others, 2)),
        dma((others,)),
        dma((others,)),
        dma((others, 2)),
        dma((others, 2)),
        dma((2, 2)),
        dma((2, 2)),
    ]
    anywhere = pl.BlockSpec(memory_space=pl.ANY)
    scalar = pl.BlockSpec(memory_space=pltpu.SMEM)
    return pl.pallas_call(
        kernel,
        out_shape=jax.ShapeDtypeStruct(transmission.shape, F32),
        in_specs=[anywhere] * 4 + [scalar] * 3 + [anywhere] * 2,
        out_specs=pl.BlockSpec(memory_space=pltpu.VMEM),
        scratch_shapes=scratch,
        compiler_params=pltpu.CompilerParams(
            collective_id=0, has_side_effects=True, vmem_limit_bytes=48 << 20
        ),
    )(transmission, probe_wave, prop_phase, measured, scan_rows, scan_cols, live_counts, t1, t2)


def solution(mesh):
    in_specs = (
        P("depth", None, "scan", None),
        P(),
        P(),
        P("scan", None, None),
        P("scan"),
        P("scan"),
        P("scan"),
    )
    out_specs = P("depth", None, "scan", None)
    return jax.shard_map(body, mesh=mesh, in_specs=in_specs, out_specs=out_specs, check_vma=False)
```

```python
import functools
import math

import jax
import jax.numpy as jnp
import numpy as np
from jax import lax
from jax.experimental import pallas as pl
from jax.experimental.pallas import tpu as pltpu
from jax.sharding import PartitionSpec as P

MESH = pl.DeviceIdType.MESH
BF16 = jnp.bfloat16
F32 = jnp.float32


def dft_blocks(pixels):
    index = np.arange(pixels)
    angles = (index[:, None] * index[None, :] % pixels) * (2.0 * math.pi / pixels)
    scale = 1.0 / math.sqrt(pixels)
    re, im = np.cos(angles) * scale, -np.sin(angles) * scale
    first = np.block([[re, -im], [im, re]])
    return jnp.asarray(first, F32).astype(BF16), jnp.asarray(first.T, F32).astype(BF16)


def kernel(
    tile_hbm, probe_hbm, phase_hbm, meas_hbm, rows_hbm, cols_hbm, live_hbm, t1_hbm, t2_hbm,
    own_hbm, got_low, got_high,
    rows_s, cols_s, live_s, blk, low, tile32, tile16, probe32, phase, meas, t1, t2, par_out, par_in,
    lower, upper, crops_b, crops_a, patch, prop, psi, xs, us, grads, came,
    strip_low, strip_high,
    load_sem, par_sem, tile_sem_s, tile_sem_r, meas_sem,
    bx_s, bx_r, ax_s, ax_r, gb_s, gb_r, ga_s, ga_r, strip_s, strip_r,
):
    depth = lax.axis_index("depth")
    scan = lax.axis_index("scan")
    n_depth = lax.axis_size("depth")
    n_scan = lax.axis_size("scan")
    after = lax.rem(scan + 1, n_scan)
    before = lax.rem(scan + n_scan - 1, n_scan)
    half, width = patch.shape[3], patch.shape[4]
    blocks = tile32.shape[2] // width
    slots = n_depth
    rows = half // 2
    chunks = [(plane, slice(part * rows, (part + 1) * rows)) for plane in range(2) for part in range(2)]

    def peer(offset):
        return (lax.rem(depth + offset, n_depth), scan)

    loads = [
        pltpu.make_async_copy(tile_hbm.at[0, 0], tile32.at[0], load_sem.at[0]),
        pltpu.make_async_copy(tile_hbm.at[0, 1], tile32.at[1], load_sem.at[1]),
        pltpu.make_async_copy(probe_hbm, probe32, load_sem.at[2]),
        pltpu.make_async_copy(phase_hbm, phase, load_sem.at[3]),
        pltpu.make_async_copy(t1_hbm, t1, load_sem.at[4]),
        pltpu.make_async_copy(t2_hbm, t2, load_sem.at[5]),
        pltpu.make_async_copy(rows_hbm, rows_s, load_sem.at[6]),
        pltpu.make_async_copy(cols_hbm, cols_s, load_sem.at[7]),
        pltpu.make_async_copy(live_hbm, live_s, load_sem.at[8]),
    ]
    for load in loads:
        load.start()

    barrier = pltpu.get_barrier_semaphore()
    for offset in range(1, n_depth):
        pl.semaphore_signal(barrier, inc=1, device_id=peer(offset), device_id_type=MESH)
    pl.semaphore_signal(barrier, inc=1, device_id=(depth, after), device_id_type=MESH)
    pl.semaphore_signal(barrier, inc=1, device_id=(depth, before), device_id_type=MESH)
    for load in loads[6:]:
        load.wait()
    for slot in range(slots):
        par_out[slot : slot + 1, :] = jnp.full((1, width), rows_s[slot], jnp.int32)
        par_out[slots + slot : slots + slot + 1, :] = jnp.full((1, width), cols_s[slot], jnp.int32)
    par_out[2 * slots : 2 * slots + 1, :] = jnp.full((1, width), live_s[0], jnp.int32)
    pl.semaphore_wait(barrier, n_depth + 1)

    def send(src, dst, s_sem, r_sem, device):
        return pltpu.make_async_remote_copy(
            src_ref=src, dst_ref=dst, send_sem=s_sem, recv_sem=r_sem,
            device_id=device, device_id_type=MESH,
        )

    par_copy = send(par_out, par_in, par_sem.at[0], par_sem.at[1], (depth, after))
    par_copy.start()
    tile_copies = []
    for at, (plane, span) in enumerate(chunks):
        if at % 2 == 0:
            loads[plane].wait()
        tile16[plane, span] = tile32[plane, span].astype(BF16)
        pair = [
            send(tile16.at[plane, span], lower.at[plane, span], tile_sem_s.at[0, at],
                 tile_sem_r.at[0, at], (depth, after)),
            send(tile16.at[plane, span], upper.at[plane, span], tile_sem_s.at[1, at],
                 tile_sem_r.at[1, at], (depth, before)),
        ]
        for copy in pair:
            copy.start()
        tile_copies.append(pair)
    meas_copy = send(meas_hbm.at[depth], meas, meas_sem.at[0], meas_sem.at[1], (depth, after))
    meas_copy.start()

    par_copy.wait_recv()
    row_at = lax.broadcasted_iota(jnp.int32, (half, width), 0)
    lane_at = lax.broadcasted_iota(jnp.int32, (rows, width), 1)
    for slot in range(slots):
        first = jnp.broadcast_to(par_in[slots + slot : slots + slot + 1, :], (rows, width))
        block = (first >> 8) + jnp.where(lane_at < (first & (width - 1)), 1, 0)
        blk[slot] = block.astype(F32).astype(BF16)
        begin = jnp.broadcast_to(par_in[slot : slot + 1, :], (half, width))
        low[slot] = jnp.where(row_at >= begin, 1.0, 0.0).astype(BF16)

    def pick(slot, values):
        piece = values[0]
        for at in range(1, blocks):
            piece = jnp.where(blk[slot] == at, values[at], piece)
        return piece

    def columns(at):
        return slice(at * width, (at + 1) * width)

    b_copies = []
    for offset in range(n_depth):
        slot = lax.rem(depth + offset, n_depth)
        for plane, span in chunks:
            piece = pick(slot, [tile16[plane, span, columns(at)] for at in range(blocks)])
            if offset == 0:
                patch[depth, 1, plane, span] = piece
            else:
                crops_b[offset - 1, plane, span] = piece
        if offset:
            copy = send(crops_b.at[offset - 1], patch.at[depth, 1], bx_s.at[offset - 1],
                        bx_r.at[offset - 1], peer(offset))
            copy.start()
            b_copies.append(copy)

    loads[2].wait()
    loads[3].wait()
    big_row = lax.broadcasted_iota(jnp.int32, (width, width), 0)
    big_lane = lax.broadcasted_iota(jnp.int32, (width, width), 1)
    own_row = jnp.broadcast_to(par_in[pl.ds(depth, 1), :], (width, width))
    own_col = jnp.broadcast_to(par_in[pl.ds(slots + depth, 1), :], (width, width))
    down = jnp.where(((big_row - own_row) & (width - 1)) == big_lane, 1.0, 0.0).astype(BF16)
    across = jnp.where(((big_row + own_col) & (width - 1)) == big_lane, 1.0, 0.0).astype(BF16)
    for plane in range(2):
        rolled = jnp.dot(down, probe32[plane].astype(BF16), preferred_element_type=F32)
        rolled = jnp.dot(rolled.astype(BF16), across, preferred_element_type=F32)
        psi[0, plane] = rolled.astype(BF16)
    prop[0] = jnp.cos(phase[...])
    prop[1] = jnp.sin(phase[...])

    a_copies = []
    for number, (plane, span) in enumerate(chunks):
        for copy in tile_copies[number]:
            copy.wait_recv()
        for offset in (1, 3, 2, 0) if n_depth == 4 else range(n_depth):
            slot = lax.rem(depth + offset, n_depth)
            is_low = low[slot, span] > 0.5
            piece = pick(slot, [
                jnp.where(is_low, lower[plane, span, columns(at)], upper[plane, span, columns(at)])
                for at in range(blocks)
            ])
            if offset == 0:
                patch[depth, 0, plane, span] = piece
            else:
                crops_a[offset - 1, plane, span] = piece
                copy = send(crops_a.at[offset - 1, plane, span], patch.at[depth, 0, plane, span],
                            ax_s.at[offset - 1, number], ax_r.at[offset - 1, number],
                            peer(offset))
                copy.start()
                a_copies.append(copy)

    loads[4].wait()
    loads[5].wait()

    def transform(left, right):
        inner = jnp.dot(left[...], xs[...], preferred_element_type=F32)
        us[:, :width] = inner[:width].astype(BF16)
        us[:, width:] = inner[width:].astype(BF16)
        both = jnp.dot(us[...], right[...], preferred_element_type=F32)
        return both[:, :width], both[:, width:]

    def keep(re, im):
        xs[:width] = re.astype(BF16)
        xs[width:] = im.astype(BF16)

    def forward(at, carry):
        @pl.when(at != depth)
        def _():
            offset = lax.rem(depth + n_depth - at, n_depth) - 1
            send(crops_b.at[offset], patch.at[at, 1], bx_s.at[offset], bx_r.at[offset],
                 (at, scan)).wait_recv()
            for number, (plane, rows_at) in enumerate(chunks):
                send(crops_a.at[offset, plane, rows_at], patch.at[at, 0, plane, rows_at],
                     ax_s.at[offset, number], ax_r.at[offset, number],
                     (at, scan)).wait_recv()

        for part in range(2):
            span = slice(part * half, (part + 1) * half)
            tr, ti = patch[at, part, 0].astype(F32), patch[at, part, 1].astype(F32)
            pr, pi = psi[at, 0, span].astype(F32), psi[at, 1, span].astype(F32)
            xs[part * half : (part + 1) * half] = (tr * pr - ti * pi).astype(BF16)
            xs[width + part * half : width + (part + 1) * half] = (tr * pi + ti * pr).astype(BF16)
        re, im = transform(t1, t2)
        keep(re * prop[0] - im * prop[1], re * prop[1] + im * prop[0])
        re, im = transform(t2, t1)
        psi[at + 1, 0] = re.astype(BF16)
        psi[at + 1, 1] = im.astype(BF16)
        return carry

    lax.fori_loop(0, n_depth, forward, 0)

    xs[:width] = psi[n_depth, 0]
    xs[width:] = psi[n_depth, 1]
    re, im = transform(t1, t2)
    meas_copy.wait_recv()
    live = jnp.where(jnp.broadcast_to(par_in[2 * slots : 2 * slots + 1, :], (width, width)) > depth, 1.0, 0.0)
    factor = live * (1.0 - meas[...] / jnp.sqrt(re * re + im * im + 1.0))
    keep(factor * re, factor * im)
    re, im = transform(t2, t1)
    keep(re, im)

    def grad_near(at):
        offset = lax.rem(at + n_depth - depth, n_depth) - 1
        return [
            send(grads.at[at, 0, plane, span], came.at[depth, 0, plane, span],
                 ga_s.at[offset, number], ga_r.at[offset, number], (at, scan))
            for number, (plane, span) in enumerate(chunks)
        ]

    def grad_far(at):
        offset = lax.rem(at + n_depth - depth, n_depth) - 1
        return send(grads.at[at, 1], came.at[depth, 1], gb_s.at[offset], gb_r.at[offset],
                    (at, scan))

    def backward(step, carry):
        at = n_depth - 1 - step
        re, im = transform(t1, t2)
        keep(re * prop[0] + im * prop[1], im * prop[0] - re * prop[1])
        mu_re, mu_im = transform(t2, t1)
        for part in range(2):
            span = slice(part * half, (part + 1) * half)
            re, im = mu_re[span], mu_im[span]
            tr, ti = patch[at, part, 0].astype(F32), patch[at, part, 1].astype(F32)
            pr, pi = psi[at, 0, span].astype(F32), psi[at, 1, span].astype(F32)
            grads[at, part, 0] = (pr * re + pi * im).astype(BF16)
            grads[at, part, 1] = (pr * im - pi * re).astype(BF16)
            xs[part * half : (part + 1) * half] = (tr * re + ti * im).astype(BF16)
            xs[width + part * half : width + (part + 1) * half] = (tr * im - ti * re).astype(BF16)

        @pl.when(at != depth)
        def _():
            for copy in grad_near(at):
                copy.start()

        return carry

    lax.fori_loop(0, n_depth, backward, 0)

    for back in range(n_depth):
        at = n_depth - 1 - back

        @pl.when(at != depth)
        def _(at=at):
            grad_far(at).start()

    for part in range(2):
        for plane in range(2):
            came[depth, part, plane] = grads[depth, part, plane]
    zero = jnp.zeros((rows // 2, width), BF16)
    strip_copies = []
    for number, (plane, span) in enumerate(chunks):
        for offset in range(n_depth - 1):
            send(grads.at[0, 0, plane, span], came.at[0, 0, plane, span], ga_s.at[offset, number],
                 ga_r.at[offset, number], (depth, scan)).wait_recv()
        for piece in range(2):
            start = span.start + piece * (rows // 2)
            at_rows = slice(start, start + rows // 2)
            lows, highs = [], []
            for slot in range(slots):
                value = came[slot, 0, plane, at_rows]
                is_low = low[slot, at_rows] > 0.5
                lows.append(jnp.where(is_low, value, zero))
                highs.append(jnp.where(is_low, zero, value))
            for at in range(blocks):
                for target, values in ((strip_low, lows), (strip_high, highs)):
                    terms = [
                        jnp.where(blk[slot, : rows // 2] == at, values[slot], zero)
                        for slot in range(slots)
                    ]
                    total = (terms[0] + terms[1]) + (terms[2] + terms[3])
                    target[plane, at_rows, columns(at)] = total
        pair = [
            send(strip_low.at[plane, span], got_low.at[plane, span], strip_s.at[0, number],
                 strip_r.at[0, number], (depth, before)),
            send(strip_high.at[plane, span], got_high.at[plane, span], strip_s.at[1, number],
                 strip_r.at[1, number], (depth, after)),
        ]
        for copy in pair:
            copy.start()
        strip_copies.append(pair)

    for offset in range(n_depth - 1):
        send(grads.at[0, 1], came.at[0, 1], gb_s.at[offset], gb_r.at[offset],
             (depth, scan)).wait_recv()
    stores = []
    for plane in range(2):
        for piece in range(4):
            at_rows = slice(piece * (rows // 2), (piece + 1) * (rows // 2))
            values = [came[slot, 1, plane, at_rows] for slot in range(slots)]
            for at in range(blocks):
                terms = [
                    jnp.where(blk[slot, : rows // 2] == at, values[slot], zero).astype(F32)
                    for slot in range(slots)
                ]
                total = (terms[0] + terms[1]) + (terms[2] + terms[3])
                tile32[plane, at_rows, columns(at)] = total
        store = pltpu.make_async_copy(tile32.at[plane], own_hbm.at[plane], load_sem.at[plane])
        store.start()
        stores.append(store)
    for pair in strip_copies:
        for copy in pair:
            copy.wait_recv()
    for store in stores:
        store.wait()

    par_copy.wait_send()
    meas_copy.wait_send()
    for copy in b_copies + a_copies:
        copy.wait_send()
    for pair in tile_copies + strip_copies:
        for copy in pair:
            copy.wait_send()
    for step in range(1, n_depth):
        at = lax.rem(depth + step, n_depth)
        for copy in grad_near(at) + [grad_far(at)]:
            copy.wait_send()


def body(transmission, probe_wave, prop_phase, measured, scan_rows, scan_cols, live_counts):
    width = probe_wave.shape[-1]
    half = transmission.shape[2]
    columns = transmission.shape[3]
    n_depth = lax.axis_size("depth")
    t1, t2 = dft_blocks(width)
    dma = pltpu.SemaphoreType.DMA
    others = n_depth - 1
    scratch = [
        pltpu.SMEM((n_depth,), jnp.int32),
        pltpu.SMEM((n_depth,), jnp.int32),
        pltpu.SMEM((1,), jnp.int32),
        pltpu.VMEM((n_depth, half // 2, width), BF16),
        pltpu.VMEM((n_depth, half, width), BF16),
        pltpu.VMEM((2, half, columns), F32),
        pltpu.VMEM((2, half, columns), BF16),
        pltpu.VMEM((2, width, width), F32),
        pltpu.VMEM((width, width), F32),
        pltpu.VMEM((width, width), F32),
        pltpu.VMEM((2 * width, 2 * width), BF16),
        pltpu.VMEM((2 * width, 2 * width), BF16),
        pltpu.VMEM((16, width), jnp.int32),
        pltpu.VMEM((16, width), jnp.int32),
        pltpu.VMEM((2, half, columns), BF16),
        pltpu.VMEM((2, half, columns), BF16),
        pltpu.VMEM((others, 2, half, width), BF16),
        pltpu.VMEM((others, 2, half, width), BF16),
        pltpu.VMEM((n_depth, 2, 2, half, width), BF16),
        pltpu.VMEM((2, width, width), F32),
        pltpu.VMEM((n_depth + 1, 2, width, width), BF16),
        pltpu.VMEM((2 * width, width), BF16),
        pltpu.VMEM((width, 2 * width), BF16),
        pltpu.VMEM((n_depth, 2, 2, half, width), BF16),
        pltpu.VMEM((n_depth, 2, 2, half, width), BF16),
        pltpu.VMEM((2, half, columns), BF16),
        pltpu.VMEM((2, half, columns), BF16),
        dma((9,)),
        dma((2,)),
        dma((2, 4)),
        dma((2, 4)),
        dma((2,)),
        dma((others,)),
        dma((others,)),
        dma((others, 4)),
        dma((others, 4)),
        dma((others,)),
        dma((others,)),
        dma((others, 4)),
        dma((others, 4)),
        dma((2, 4)),
        dma((2, 4)),
    ]
    anywhere = pl.BlockSpec(memory_space=pltpu.HBM)
    own, from_after, from_before = pl.pallas_call(
        kernel,
        out_shape=[
            jax.ShapeDtypeStruct((2, half, columns), F32),
            jax.ShapeDtypeStruct((2, half, columns), BF16),
            jax.ShapeDtypeStruct((2, half, columns), BF16),
        ],
        in_specs=[anywhere] * 9,
        out_specs=[anywhere] * 3,
        scratch_shapes=scratch,
        compiler_params=pltpu.CompilerParams(
            collective_id=0, has_side_effects=True, vmem_limit_bytes=67_000_000
        ),
    )(transmission, probe_wave, prop_phase, measured, scan_rows, scan_cols, live_counts, t1, t2)
    return (own + from_after.astype(F32) + from_before.astype(F32))[None]


def solution(mesh):
    in_specs = (
        P("depth", None, "scan", None),
        P(),
        P(),
        P("scan", None, None),
        P("scan"),
        P("scan"),
        P("scan"),
    )
    out_specs = P("depth", None, "scan", None)
    return jax.shard_map(body, mesh=mesh, in_specs=in_specs, out_specs=out_specs, check_vma=False)
```

```python
import functools
import math

import jax
import jax.numpy as jnp
import numpy as np
from jax import lax
from jax.experimental import pallas as pl
from jax.experimental.pallas import tpu as pltpu
from jax.sharding import PartitionSpec as P

MESH = pl.DeviceIdType.MESH
BF16 = jnp.bfloat16
F32 = jnp.float32


def dft_blocks(pixels):
    index = np.arange(pixels)
    angles = (index[:, None] * index[None, :] % pixels) * (2.0 * math.pi / pixels)
    scale = 1.0 / math.sqrt(pixels)
    re, im = np.cos(angles) * scale, -np.sin(angles) * scale
    blocks = []
    for parity in range(2):
        r, i = re[parity::2, : pixels // 2], im[parity::2, : pixels // 2]
        blocks.append(np.block([[r, -i], [i, r]]))
    blocks = np.stack(blocks)
    return jnp.asarray(blocks, F32).astype(BF16), jnp.asarray(blocks.swapaxes(1, 2), F32).astype(BF16)


def kernel(
    tile_hbm, probe_hbm, phase_hbm, meas_hbm, rows_hbm, cols_hbm, live_hbm, t1_hbm, t2_hbm,
    out_hbm,
    rows_s, cols_s, live_s, blk, low, tile32, tile16, probe32, phase, meas_in, meas_out, meas, t1, t2, par_out, par_in,
    lower, upper, crops_b, crops_a, patch, prop, psi, adjoint, xs, us, grads, came,
    strip_low, strip_high, got_low, got_high,
    load_sem, par_sem, tile_sem_s, tile_sem_r, meas_sem,
    bx_s, bx_r, ax_s, ax_r, gb_s, gb_r, ga_s, ga_r, strip_s, strip_r,
):
    depth = lax.axis_index("depth")
    scan = lax.axis_index("scan")
    n_depth = lax.axis_size("depth")
    n_scan = lax.axis_size("scan")
    after = lax.rem(scan + 1, n_scan)
    before = lax.rem(scan + n_scan - 1, n_scan)
    half, width = patch.shape[3], patch.shape[4]
    blocks = tile32.shape[2] // width
    slots = n_depth
    rows = half // 2
    chunks = [(plane, slice(part * rows, (part + 1) * rows)) for plane in range(2) for part in range(2)]

    def peer(offset):
        return (lax.rem(depth + offset, n_depth), scan)

    loads = [
        pltpu.make_async_copy(tile_hbm.at[0, 0], tile32.at[0], load_sem.at[0]),
        pltpu.make_async_copy(tile_hbm.at[0, 1], tile32.at[1], load_sem.at[1]),
        pltpu.make_async_copy(probe_hbm, probe32, load_sem.at[2]),
        pltpu.make_async_copy(phase_hbm, phase, load_sem.at[3]),
        pltpu.make_async_copy(t1_hbm, t1, load_sem.at[4]),
        pltpu.make_async_copy(t2_hbm, t2, load_sem.at[5]),
        pltpu.make_async_copy(rows_hbm, rows_s, load_sem.at[6]),
        pltpu.make_async_copy(cols_hbm, cols_s, load_sem.at[7]),
        pltpu.make_async_copy(live_hbm, live_s, load_sem.at[8]),
        pltpu.make_async_copy(meas_hbm.at[depth], meas_in, load_sem.at[9]),
    ]
    for at in (6, 7, 8, 0, 1, 9, 3, 2, 4, 5):
        loads[at].start()

    barrier = pltpu.get_barrier_semaphore()
    for offset in range(1, n_depth):
        pl.semaphore_signal(barrier, inc=1, device_id=peer(offset), device_id_type=MESH)
    pl.semaphore_signal(barrier, inc=1, device_id=(depth, after), device_id_type=MESH)
    pl.semaphore_signal(barrier, inc=1, device_id=(depth, before), device_id_type=MESH)
    for load in loads[6:9]:
        load.wait()
    for slot in range(slots):
        par_out[slot : slot + 1, :] = jnp.full((1, width), rows_s[slot], jnp.int32)
        par_out[slots + slot : slots + slot + 1, :] = jnp.full((1, width), cols_s[slot], jnp.int32)
    par_out[2 * slots : 2 * slots + 1, :] = jnp.full((1, width), live_s[0], jnp.int32)
    pl.semaphore_wait(barrier, n_depth + 1)

    def send(src, dst, s_sem, r_sem, device):
        return pltpu.make_async_remote_copy(
            src_ref=src, dst_ref=dst, send_sem=s_sem, recv_sem=r_sem,
            device_id=device, device_id_type=MESH,
        )

    par_copy = send(par_out, par_in, par_sem.at[0], par_sem.at[1], (depth, after))
    par_copy.start()
    tile_copies = []
    for at, (plane, span) in enumerate(chunks):
        if at % 2 == 0:
            loads[plane].wait()
        tile16[plane, span] = tile32[plane, span].astype(BF16)
        pair = [
            send(tile16.at[plane, span], lower.at[plane, span], tile_sem_s.at[0, at],
                 tile_sem_r.at[0, at], (depth, after)),
            send(tile16.at[plane, span], upper.at[plane, span], tile_sem_s.at[1, at],
                 tile_sem_r.at[1, at], (depth, before)),
        ]
        for copy in pair:
            copy.start()
        tile_copies.append(pair)
    par_copy.wait_recv()
    row_at = lax.broadcasted_iota(jnp.int32, (half, width), 0)
    lane_at = lax.broadcasted_iota(jnp.int32, (rows, width), 1)
    for slot in range(slots):
        first = jnp.broadcast_to(par_in[slots + slot : slots + slot + 1, :], (rows, width))
        block = (first >> 8) + jnp.where(lane_at < (first & (width - 1)), 1, 0)
        blk[slot] = block.astype(F32).astype(BF16)
        begin = jnp.broadcast_to(par_in[slot : slot + 1, :], (half, width))
        low[slot] = jnp.where(row_at >= begin, 1.0, 0.0).astype(BF16)

    def pick(slot, values):
        piece = values[0]
        for at in range(1, blocks):
            piece = jnp.where(blk[slot] == at, values[at], piece)
        return piece

    def columns(at):
        return slice(at * width, (at + 1) * width)

    b_copies = []
    for offset in range(n_depth):
        slot = lax.rem(depth + offset, n_depth)
        for plane, span in chunks:
            piece = pick(slot, [tile16[plane, span, columns(at)] for at in range(blocks)])
            if offset == 0:
                patch[depth, 1, plane, span] = piece
            else:
                crops_b[offset - 1, plane, span] = piece
        if offset:
            copy = send(crops_b.at[offset - 1], patch.at[depth, 1], bx_s.at[offset - 1],
                        bx_r.at[offset - 1], peer(offset))
            copy.start()
            b_copies.append(copy)

    big_row = lax.broadcasted_iota(jnp.int32, (width, width), 0)
    big_lane = lax.broadcasted_iota(jnp.int32, (width, width), 1)
    to_split = jnp.where(2 * (big_row & (half - 1)) + (big_row // half) == big_lane, 1.0, 0.0).astype(BF16)
    of_split = jnp.where(2 * (big_lane & (half - 1)) + (big_lane // half) == big_row, 1.0, 0.0).astype(BF16)

    def split_order(value, parts):
        total = jnp.zeros_like(value)
        for _ in range(parts):
            part = value.astype(BF16)
            value = value - part.astype(F32)
            moved = jnp.dot(to_split, part, preferred_element_type=F32).astype(BF16)
            total = total + jnp.dot(moved, of_split, preferred_element_type=F32)
        return total

    loads[9].wait()
    meas_out[...] = split_order(meas_in[...], 3)
    meas_copy = send(meas_out, meas, meas_sem.at[0], meas_sem.at[1], (depth, after))
    meas_copy.start()
    loads[3].wait()
    phase[...] = split_order(phase[...], 3)
    prop[0] = jnp.cos(phase[...])

    loads[2].wait()
    own_row = jnp.broadcast_to(par_in[pl.ds(depth, 1), :], (width, width))
    own_col = jnp.broadcast_to(par_in[pl.ds(slots + depth, 1), :], (width, width))
    down = jnp.where(((big_row - own_row) & (width - 1)) == big_lane, 1.0, 0.0).astype(BF16)
    across = jnp.where(((big_row + own_col) & (width - 1)) == big_lane, 1.0, 0.0).astype(BF16)
    for plane in range(2):
        rolled = jnp.dot(down, probe32[plane].astype(BF16), preferred_element_type=F32)
        rolled = jnp.dot(rolled.astype(BF16), across, preferred_element_type=F32)
        psi[0, plane] = rolled.astype(BF16)

    a_copies = []
    for number, (plane, span) in enumerate(chunks):
        for copy in tile_copies[number]:
            copy.wait_recv()
        for offset in (1, 3, 2, 0) if n_depth == 4 else range(n_depth):
            slot = lax.rem(depth + offset, n_depth)
            is_low = low[slot, span] > 0.5
            piece = pick(slot, [
                jnp.where(is_low, lower[plane, span, columns(at)], upper[plane, span, columns(at)])
                for at in range(blocks)
            ])
            if offset == 0:
                patch[depth, 0, plane, span] = piece
            else:
                crops_a[offset - 1, plane, span] = piece
                copy = send(crops_a.at[offset - 1, plane, span], patch.at[depth, 0, plane, span],
                            ax_s.at[offset - 1, number], ax_r.at[offset - 1, number],
                            peer(offset))
                copy.start()
                a_copies.append(copy)

    prop[1] = jnp.sin(phase[...])
    loads[4].wait()
    loads[5].wait()
    sides = [slice(0, half), slice(half, width)]

    def to_frequencies(upper_re, upper_im, lower_re, lower_im):
        xs[0, :half] = (upper_re + lower_re).astype(BF16)
        xs[0, half:] = (upper_im + lower_im).astype(BF16)
        xs[1, :half] = (upper_re - lower_re).astype(BF16)
        xs[1, half:] = (upper_im - lower_im).astype(BF16)
        for parity in range(2):
            inner = jnp.dot(t1[parity], xs[parity], preferred_element_type=F32)
            for part in range(2):
                left, right = inner[sides[part], :half], inner[sides[part], half:]
                us[0, sides[parity], sides[part]] = (left + right).astype(BF16)
                us[1, sides[parity], sides[part]] = (left - right).astype(BF16)
        return [
            jnp.dot(us[parity], t2[parity], preferred_element_type=F32) for parity in range(2)
        ]

    def keep(parity, re, im):
        for part in range(2):
            xs[part, :half, sides[parity]] = re[sides[part]].astype(BF16)
            xs[part, half:, sides[parity]] = im[sides[part]].astype(BF16)

    def to_positions():
        even = jnp.dot(t2[0], xs[0], preferred_element_type=F32)
        odd = jnp.dot(t2[1], xs[1], preferred_element_type=F32)
        for part in range(2):
            upper_half = (even[sides[part]] + odd[sides[part]]).astype(BF16)
            lower_half = (even[sides[part]] - odd[sides[part]]).astype(BF16)
            for parity in range(2):
                us[parity, :half, sides[part]] = upper_half[:, sides[parity]]
                us[parity, half:, sides[part]] = lower_half[:, sides[parity]]
        even = jnp.dot(us[0], t1[0], preferred_element_type=F32)
        odd = jnp.dot(us[1], t1[1], preferred_element_type=F32)
        return [
            jnp.concatenate([even[:, side] + odd[:, side], even[:, side] - odd[:, side]], axis=1)
            for side in sides
        ]

    def propagate(halves, sign):
        both = to_frequencies(*halves)
        for parity in range(2):
            re, im = both[parity][:, :half], both[parity][:, half:]
            pr, pi = prop[0, :, sides[parity]], sign * prop[1, :, sides[parity]]
            keep(parity, re * pr - im * pi, re * pi + im * pr)
        return to_positions()

    def forward(at, carry):
        @pl.when(at != depth)
        def _():
            offset = lax.rem(depth + n_depth - at, n_depth) - 1
            send(crops_b.at[offset], patch.at[at, 1], bx_s.at[offset], bx_r.at[offset],
                 (at, scan)).wait_recv()
            for number, (plane, rows_at) in enumerate(chunks):
                send(crops_a.at[offset, plane, rows_at], patch.at[at, 0, plane, rows_at],
                     ax_s.at[offset, number], ax_r.at[offset, number],
                     (at, scan)).wait_recv()

        halves = []
        for part in range(2):
            tr, ti = patch[at, part, 0].astype(F32), patch[at, part, 1].astype(F32)
            pr, pi = psi[at, 0, sides[part]].astype(F32), psi[at, 1, sides[part]].astype(F32)
            halves += [tr * pr - ti * pi, tr * pi + ti * pr]
        re, im = propagate(halves, 1.0)
        psi[at + 1, 0] = re.astype(BF16)
        psi[at + 1, 1] = im.astype(BF16)
        return carry

    lax.fori_loop(0, n_depth, forward, 0)

    leaving = [psi[n_depth, plane, side].astype(F32) for side in sides for plane in range(2)]
    both = to_frequencies(*leaving)
    meas_copy.wait_recv()
    live = jnp.where(
        jnp.broadcast_to(par_in[2 * slots : 2 * slots + 1, :half], (width, half)) > depth, 1.0, 0.0
    )
    for parity in range(2):
        re, im = both[parity][:, :half], both[parity][:, half:]
        factor = live * (1.0 - meas[:, sides[parity]] / jnp.sqrt(re * re + im * im + 1.0))
        keep(parity, factor * re, factor * im)
    re, im = to_positions()
    adjoint[0] = re
    adjoint[1] = im

    def grad_near(at):
        offset = lax.rem(at + n_depth - depth, n_depth) - 1
        return [
            send(grads.at[at, 0, plane, span], came.at[depth, 0, plane, span],
                 ga_s.at[offset, number], ga_r.at[offset, number], (at, scan))
            for number, (plane, span) in enumerate(chunks)
        ]

    def grad_far(at):
        offset = lax.rem(at + n_depth - depth, n_depth) - 1
        return send(grads.at[at, 1], came.at[depth, 1], gb_s.at[offset], gb_r.at[offset],
                    (at, scan))

    def backward(step, carry):
        at = n_depth - 1 - step
        mu_re, mu_im = propagate([adjoint[plane, side] for side in sides for plane in range(2)], -1.0)
        for part in range(2):
            re, im = mu_re[sides[part]], mu_im[sides[part]]
            tr, ti = patch[at, part, 0].astype(F32), patch[at, part, 1].astype(F32)
            pr, pi = psi[at, 0, sides[part]].astype(F32), psi[at, 1, sides[part]].astype(F32)
            grads[at, part, 0] = (pr * re + pi * im).astype(BF16)
            grads[at, part, 1] = (pr * im - pi * re).astype(BF16)
            adjoint[0, sides[part]] = tr * re + ti * im
            adjoint[1, sides[part]] = tr * im - ti * re

        @pl.when(at != depth)
        def _():
            for copy in grad_near(at):
                copy.start()

        return carry

    lax.fori_loop(0, n_depth, backward, 0)

    for back in range(n_depth):
        at = n_depth - 1 - back

        @pl.when(at != depth)
        def _(at=at):
            grad_far(at).start()

    for part in range(2):
        for plane in range(2):
            came[depth, part, plane] = grads[depth, part, plane]
    zero = jnp.zeros((rows // 2, width), BF16)
    strip_copies = []
    for number, (plane, span) in enumerate(chunks):
        for offset in range(n_depth - 1):
            send(grads.at[0, 0, plane, span], came.at[0, 0, plane, span], ga_s.at[offset, number],
                 ga_r.at[offset, number], (depth, scan)).wait_recv()
        for piece in range(2):
            start = span.start + piece * (rows // 2)
            at_rows = slice(start, start + rows // 2)
            lows, highs = [], []
            for slot in range(slots):
                value = came[slot, 0, plane, at_rows]
                is_low = low[slot, at_rows] > 0.5
                lows.append(jnp.where(is_low, value, zero))
                highs.append(jnp.where(is_low, zero, value))
            for at in range(blocks):
                for target, values in ((strip_low, lows), (strip_high, highs)):
                    terms = [
                        jnp.where(blk[slot, : rows // 2] == at, values[slot], zero)
                        for slot in range(slots)
                    ]
                    total = (terms[0] + terms[1]) + (terms[2] + terms[3])
                    target[plane, at_rows, columns(at)] = total
        pair = [
            send(strip_low.at[plane, span], got_low.at[plane, span], strip_s.at[0, number],
                 strip_r.at[0, number], (depth, before)),
            send(strip_high.at[plane, span], got_high.at[plane, span], strip_s.at[1, number],
                 strip_r.at[1, number], (depth, after)),
        ]
        for copy in pair:
            copy.start()
        strip_copies.append(pair)

    for offset in range(n_depth - 1):
        send(grads.at[0, 1], came.at[0, 1], gb_s.at[offset], gb_r.at[offset],
             (depth, scan)).wait_recv()
    stores = []
    for plane in range(2):
        for piece in range(4):
            at_rows = slice(piece * (rows // 2), (piece + 1) * (rows // 2))
            values = [came[slot, 1, plane, at_rows] for slot in range(slots)]
            for at in range(blocks):
                terms = [
                    jnp.where(blk[slot, : rows // 2] == at, values[slot], zero).astype(F32)
                    for slot in range(slots)
                ]
                total = (terms[0] + terms[1]) + (terms[2] + terms[3])
                tile32[plane, at_rows, columns(at)] = total
    for number, (plane, span) in enumerate(chunks):
        for copy in strip_copies[number]:
            copy.wait_recv()
        tile32[plane, span] = tile32[plane, span] + (
            got_low[plane, span].astype(F32) + got_high[plane, span].astype(F32)
        )
        store = pltpu.make_async_copy(
            tile32.at[plane, span], out_hbm.at[0, plane, span], load_sem.at[number]
        )
        store.start()
        stores.append(store)
    for store in stores:
        store.wait()

    par_copy.wait_send()
    meas_copy.wait_send()
    for copy in b_copies + a_copies:
        copy.wait_send()
    for pair in tile_copies + strip_copies:
        for copy in pair:
            copy.wait_send()
    for step in range(1, n_depth):
        at = lax.rem(depth + step, n_depth)
        for copy in grad_near(at) + [grad_far(at)]:
            copy.wait_send()


def body(transmission, probe_wave, prop_phase, measured, scan_rows, scan_cols, live_counts):
    width = probe_wave.shape[-1]
    half = transmission.shape[2]
    columns = transmission.shape[3]
    n_depth = lax.axis_size("depth")
    t1, t2 = dft_blocks(width)
    dma = pltpu.SemaphoreType.DMA
    others = n_depth - 1
    scratch = [
        pltpu.SMEM((n_depth,), jnp.int32),
        pltpu.SMEM((n_depth,), jnp.int32),
        pltpu.SMEM((1,), jnp.int32),
        pltpu.VMEM((n_depth, half // 2, width), BF16),
        pltpu.VMEM((n_depth, half, width), BF16),
        pltpu.VMEM((2, half, columns), F32),
        pltpu.VMEM((2, half, columns), BF16),
        pltpu.VMEM((2, width, width), F32),
        pltpu.VMEM((width, width), F32),
        pltpu.VMEM((width, width), F32),
        pltpu.VMEM((width, width), F32),
        pltpu.VMEM((width, width), F32),
        pltpu.VMEM((2, width, width), BF16),
        pltpu.VMEM((2, width, width), BF16),
        pltpu.VMEM((16, width), jnp.int32),
        pltpu.VMEM((16, width), jnp.int32),
        pltpu.VMEM((2, half, columns), BF16),
        pltpu.VMEM((2, half, columns), BF16),
        pltpu.VMEM((others, 2, half, width), BF16),
        pltpu.VMEM((others, 2, half, width), BF16),
        pltpu.VMEM((n_depth, 2, 2, half, width), BF16),
        pltpu.VMEM((2, width, width), F32),
        pltpu.VMEM((n_depth + 1, 2, width, width), BF16),
        pltpu.VMEM((2, width, width), F32),
        pltpu.VMEM((2, width, width), BF16),
        pltpu.VMEM((2, width, width), BF16),
        pltpu.VMEM((n_depth, 2, 2, half, width), BF16),
        pltpu.VMEM((n_depth, 2, 2, half, width), BF16),
        pltpu.VMEM((2, half, columns), BF16),
        pltpu.VMEM((2, half, columns), BF16),
        pltpu.VMEM((2, half, columns), BF16),
        pltpu.VMEM((2, half, columns), BF16),
        dma((10,)),
        dma((2,)),
        dma((2, 4)),
        dma((2, 4)),
        dma((2,)),
        dma((others,)),
        dma((others,)),
        dma((others, 4)),
        dma((others, 4)),
        dma((others,)),
        dma((others,)),
        dma((others, 4)),
        dma((others, 4)),
        dma((2, 4)),
        dma((2, 4)),
    ]
    anywhere = pl.BlockSpec(memory_space=pltpu.HBM)
    return pl.pallas_call(
        kernel,
        out_shape=jax.ShapeDtypeStruct(transmission.shape, F32),
        in_specs=[anywhere] * 9,
        out_specs=anywhere,
        scratch_shapes=scratch,
        compiler_params=pltpu.CompilerParams(
            collective_id=0, has_side_effects=True, vmem_limit_bytes=67_000_000
        ),
    )(transmission, probe_wave, prop_phase, measured, scan_rows, scan_cols, live_counts, t1, t2)


def solution(mesh):
    in_specs = (
        P("depth", None, "scan", None),
        P(),
        P(),
        P("scan", None, None),
        P("scan"),
        P("scan"),
        P("scan"),
    )
    out_specs = P("depth", None, "scan", None)
    return jax.shard_map(body, mesh=mesh, in_specs=in_specs, out_specs=out_specs, check_vma=False)
```

```python
import functools
import math

import jax
import jax.numpy as jnp
import numpy as np
from jax import lax
from jax.experimental import pallas as pl
from jax.experimental.pallas import tpu as pltpu
from jax.sharding import PartitionSpec as P

MESH = pl.DeviceIdType.MESH
BF16 = jnp.bfloat16
F32 = jnp.float32


def dft_blocks(pixels):
    index = np.arange(pixels)
    angles = (index[:, None] * index[None, :] % pixels) * (2.0 * math.pi / pixels)
    scale = 1.0 / math.sqrt(pixels)
    re, im = np.cos(angles) * scale, -np.sin(angles) * scale
    blocks = []
    for parity in range(2):
        r, i = re[parity::2, : pixels // 2], im[parity::2, : pixels // 2]
        blocks.append(np.block([[r, -i], [i, r]]))
    blocks = np.stack(blocks)
    return jnp.asarray(blocks, F32).astype(BF16), jnp.asarray(blocks.swapaxes(1, 2), F32).astype(BF16)


def kernel(
    tile_hbm, probe_hbm, phase_hbm, meas_hbm, rows_hbm, cols_hbm, live_hbm, t1_hbm, t2_hbm,
    out_ref,
    rows_s, cols_s, live_s, blk, low, tile32, tile16, probe32, phase, meas_in, meas_out, meas, t1, t2, par_out, par_in,
    lower, upper, crops_b, crops_a, patch, prop, psi, adjoint, xs, us, grads, came,
    strip_low, strip_high, got_low, got_high,
    load_sem, par_sem, tile_sem_s, tile_sem_r, meas_sem,
    bx_s, bx_r, ax_s, ax_r, gb_s, gb_r, ga_s, ga_r, strip_s, strip_r,
):
    depth = lax.axis_index("depth")
    scan = lax.axis_index("scan")
    n_depth = lax.axis_size("depth")
    n_scan = lax.axis_size("scan")
    after = lax.rem(scan + 1, n_scan)
    before = lax.rem(scan + n_scan - 1, n_scan)
    half, width = patch.shape[3], patch.shape[4]
    blocks = tile32.shape[2] // width
    slots = n_depth
    rows = half // 2
    chunks = [(plane, slice(part * rows, (part + 1) * rows)) for plane in range(2) for part in range(2)]

    def peer(offset):
        return (lax.rem(depth + offset, n_depth), scan)

    loads = [
        pltpu.make_async_copy(tile_hbm.at[0, 0], tile32.at[0], load_sem.at[0]),
        pltpu.make_async_copy(tile_hbm.at[0, 1], tile32.at[1], load_sem.at[1]),
        pltpu.make_async_copy(probe_hbm, probe32, load_sem.at[2]),
        pltpu.make_async_copy(phase_hbm, phase, load_sem.at[3]),
        pltpu.make_async_copy(t1_hbm, t1, load_sem.at[4]),
        pltpu.make_async_copy(t2_hbm, t2, load_sem.at[5]),
        pltpu.make_async_copy(rows_hbm, rows_s, load_sem.at[6]),
        pltpu.make_async_copy(cols_hbm, cols_s, load_sem.at[7]),
        pltpu.make_async_copy(live_hbm, live_s, load_sem.at[8]),
        pltpu.make_async_copy(meas_hbm.at[depth], meas_in, load_sem.at[9]),
    ]
    for at in (6, 7, 8, 0, 1, 9, 3, 2, 4, 5):
        loads[at].start()

    barrier = pltpu.get_barrier_semaphore()
    for offset in range(1, n_depth):
        pl.semaphore_signal(barrier, inc=1, device_id=peer(offset), device_id_type=MESH)
    pl.semaphore_signal(barrier, inc=1, device_id=(depth, after), device_id_type=MESH)
    pl.semaphore_signal(barrier, inc=1, device_id=(depth, before), device_id_type=MESH)
    for load in loads[6:9]:
        load.wait()
    for slot in range(slots):
        par_out[slot : slot + 1, :] = jnp.full((1, width), rows_s[slot], jnp.int32)
        par_out[slots + slot : slots + slot + 1, :] = jnp.full((1, width), cols_s[slot], jnp.int32)
    par_out[2 * slots : 2 * slots + 1, :] = jnp.full((1, width), live_s[0], jnp.int32)
    pl.semaphore_wait(barrier, n_depth + 1)

    def send(src, dst, s_sem, r_sem, device):
        return pltpu.make_async_remote_copy(
            src_ref=src, dst_ref=dst, send_sem=s_sem, recv_sem=r_sem,
            device_id=device, device_id_type=MESH,
        )

    par_copy = send(par_out, par_in, par_sem.at[0], par_sem.at[1], (depth, after))
    par_copy.start()
    tile_copies = []
    for at, (plane, span) in enumerate(chunks):
        if at % 2 == 0:
            loads[plane].wait()
        tile16[plane, span] = tile32[plane, span].astype(BF16)
        pair = [
            send(tile16.at[plane, span], lower.at[plane, span], tile_sem_s.at[0, at],
                 tile_sem_r.at[0, at], (depth, after)),
            send(tile16.at[plane, span], upper.at[plane, span], tile_sem_s.at[1, at],
                 tile_sem_r.at[1, at], (depth, before)),
        ]
        for copy in pair:
            copy.start()
        tile_copies.append(pair)
    par_copy.wait_recv()
    row_at = lax.broadcasted_iota(jnp.int32, (half, width), 0)
    lane_at = lax.broadcasted_iota(jnp.int32, (rows, width), 1)
    for slot in range(slots):
        first = jnp.broadcast_to(par_in[slots + slot : slots + slot + 1, :], (rows, width))
        block = (first >> 8) + jnp.where(lane_at < (first & (width - 1)), 1, 0)
        blk[slot] = block.astype(F32).astype(BF16)
        begin = jnp.broadcast_to(par_in[slot : slot + 1, :], (half, width))
        low[slot] = jnp.where(row_at >= begin, 1.0, 0.0).astype(BF16)

    def pick(slot, values):
        piece = values[0]
        for at in range(1, blocks):
            piece = jnp.where(blk[slot] == at, values[at], piece)
        return piece

    def columns(at):
        return slice(at * width, (at + 1) * width)

    b_copies = []
    for offset in (*range(1, n_depth), 0):
        slot = lax.rem(depth + offset, n_depth)
        for plane, span in chunks:
            piece = pick(slot, [tile16[plane, span, columns(at)] for at in range(blocks)])
            if offset == 0:
                patch[depth, 1, plane, span] = piece
            else:
                crops_b[offset - 1, plane, span] = piece
        if offset:
            copy = send(crops_b.at[offset - 1], patch.at[depth, 1], bx_s.at[offset - 1],
                        bx_r.at[offset - 1], peer(offset))
            copy.start()
            b_copies.append(copy)

    big_row = lax.broadcasted_iota(jnp.int32, (width, width), 0)
    big_lane = lax.broadcasted_iota(jnp.int32, (width, width), 1)
    to_split = jnp.where(2 * (big_row & (half - 1)) + (big_row // half) == big_lane, 1.0, 0.0).astype(BF16)
    of_split = jnp.where(2 * (big_lane & (half - 1)) + (big_lane // half) == big_row, 1.0, 0.0).astype(BF16)

    def split_order(value, parts):
        total = jnp.zeros_like(value)
        for _ in range(parts):
            part = value.astype(BF16)
            value = value - part.astype(F32)
            moved = jnp.dot(to_split, part, preferred_element_type=F32).astype(BF16)
            total = total + jnp.dot(moved, of_split, preferred_element_type=F32)
        return total

    loads[9].wait()
    meas_out[...] = split_order(meas_in[...], 3)
    meas_copy = send(meas_out, meas, meas_sem.at[0], meas_sem.at[1], (depth, after))
    meas_copy.start()
    loads[3].wait()
    phase[...] = split_order(phase[...], 3)
    prop[0] = jnp.cos(phase[...])

    loads[2].wait()
    own_row = jnp.broadcast_to(par_in[pl.ds(depth, 1), :], (width, width))
    own_col = jnp.broadcast_to(par_in[pl.ds(slots + depth, 1), :], (width, width))
    down = jnp.where(((big_row - own_row) & (width - 1)) == big_lane, 1.0, 0.0).astype(BF16)
    across = jnp.where(((big_row + own_col) & (width - 1)) == big_lane, 1.0, 0.0).astype(BF16)
    for plane in range(2):
        rolled = jnp.dot(down, probe32[plane].astype(BF16), preferred_element_type=F32)
        rolled = jnp.dot(rolled.astype(BF16), across, preferred_element_type=F32)
        psi[0, plane] = rolled.astype(BF16)

    a_copies = []
    for number, (plane, span) in enumerate(chunks):
        for copy in tile_copies[number]:
            copy.wait_recv()
        for offset in (*range(1, n_depth), 0):
            slot = lax.rem(depth + offset, n_depth)
            is_low = low[slot, span] > 0.5
            piece = pick(slot, [
                jnp.where(is_low, lower[plane, span, columns(at)], upper[plane, span, columns(at)])
                for at in range(blocks)
            ])
            if offset == 0:
                patch[depth, 0, plane, span] = piece
            else:
                crops_a[offset - 1, plane, span] = piece
                copy = send(crops_a.at[offset - 1, plane, span], patch.at[depth, 0, plane, span],
                            ax_s.at[offset - 1, number], ax_r.at[offset - 1, number],
                            peer(offset))
                copy.start()
                a_copies.append(copy)

    prop[1] = jnp.sin(phase[...])
    loads[4].wait()
    loads[5].wait()
    sides = [slice(0, half), slice(half, width)]

    def to_frequencies(upper_re, upper_im, lower_re, lower_im):
        xs[0, :half] = (upper_re + lower_re).astype(BF16)
        xs[0, half:] = (upper_im + lower_im).astype(BF16)
        xs[1, :half] = (upper_re - lower_re).astype(BF16)
        xs[1, half:] = (upper_im - lower_im).astype(BF16)
        for parity in range(2):
            inner = jnp.dot(t1[parity], xs[parity], preferred_element_type=F32)
            for part in range(2):
                left, right = inner[sides[part], :half], inner[sides[part], half:]
                us[0, sides[parity], sides[part]] = (left + right).astype(BF16)
                us[1, sides[parity], sides[part]] = (left - right).astype(BF16)
        return [
            jnp.dot(us[parity], t2[parity], preferred_element_type=F32) for parity in range(2)
        ]

    def keep(parity, re, im):
        for part in range(2):
            xs[part, :half, sides[parity]] = re[sides[part]].astype(BF16)
            xs[part, half:, sides[parity]] = im[sides[part]].astype(BF16)

    def to_positions():
        even = jnp.dot(t2[0], xs[0], preferred_element_type=F32)
        odd = jnp.dot(t2[1], xs[1], preferred_element_type=F32)
        for part in range(2):
            upper_half = (even[sides[part]] + odd[sides[part]]).astype(BF16)
            lower_half = (even[sides[part]] - odd[sides[part]]).astype(BF16)
            for parity in range(2):
                us[parity, :half, sides[part]] = upper_half[:, sides[parity]]
                us[parity, half:, sides[part]] = lower_half[:, sides[parity]]
        even = jnp.dot(us[0], t1[0], preferred_element_type=F32)
        odd = jnp.dot(us[1], t1[1], preferred_element_type=F32)
        return [
            jnp.concatenate([even[:, side] + odd[:, side], even[:, side] - odd[:, side]], axis=1)
            for side in sides
        ]

    def propagate(halves, sign):
        both = to_frequencies(*halves)
        for parity in range(2):
            re, im = both[parity][:, :half], both[parity][:, half:]
            pr, pi = prop[0, :, sides[parity]], sign * prop[1, :, sides[parity]]
            keep(parity, re * pr - im * pi, re * pi + im * pr)
        return to_positions()

    def forward(at, carry):
        @pl.when(at != depth)
        def _():
            offset = lax.rem(depth + n_depth - at, n_depth) - 1
            send(crops_b.at[offset], patch.at[at, 1], bx_s.at[offset], bx_r.at[offset],
                 (at, scan)).wait_recv()
            for number, (plane, rows_at) in enumerate(chunks):
                send(crops_a.at[offset, plane, rows_at], patch.at[at, 0, plane, rows_at],
                     ax_s.at[offset, number], ax_r.at[offset, number],
                     (at, scan)).wait_recv()

        halves = []
        for part in range(2):
            tr, ti = patch[at, part, 0].astype(F32), patch[at, part, 1].astype(F32)
            pr, pi = psi[at, 0, sides[part]].astype(F32), psi[at, 1, sides[part]].astype(F32)
            halves += [tr * pr - ti * pi, tr * pi + ti * pr]
        re, im = propagate(halves, 1.0)
        psi[at + 1, 0] = re.astype(BF16)
        psi[at + 1, 1] = im.astype(BF16)
        return carry

    lax.fori_loop(0, n_depth, forward, 0)

    leaving = [psi[n_depth, plane, side].astype(F32) for side in sides for plane in range(2)]
    both = to_frequencies(*leaving)
    meas_copy.wait_recv()
    live = jnp.where(
        jnp.broadcast_to(par_in[2 * slots : 2 * slots + 1, :half], (width, half)) > depth, 1.0, 0.0
    )
    for parity in range(2):
        re, im = both[parity][:, :half], both[parity][:, half:]
        factor = live * (1.0 - meas[:, sides[parity]] / jnp.sqrt(re * re + im * im + 1.0))
        keep(parity, factor * re, factor * im)
    re, im = to_positions()
    adjoint[0] = re
    adjoint[1] = im

    def grad_near(at):
        offset = lax.rem(at + n_depth - depth, n_depth) - 1
        return [
            send(grads.at[at, 0, plane, span], came.at[depth, 0, plane, span],
                 ga_s.at[offset, number], ga_r.at[offset, number], (at, scan))
            for number, (plane, span) in enumerate(chunks)
        ]

    def grad_far(at):
        offset = lax.rem(at + n_depth - depth, n_depth) - 1
        return send(grads.at[at, 1], came.at[depth, 1], gb_s.at[offset], gb_r.at[offset],
                    (at, scan))

    def backward(step, carry):
        at = n_depth - 1 - step
        mu_re, mu_im = propagate([adjoint[plane, side] for side in sides for plane in range(2)], -1.0)
        for part in range(2):
            re, im = mu_re[sides[part]], mu_im[sides[part]]
            tr, ti = patch[at, part, 0].astype(F32), patch[at, part, 1].astype(F32)
            pr, pi = psi[at, 0, sides[part]].astype(F32), psi[at, 1, sides[part]].astype(F32)
            grads[at, part, 0] = (pr * re + pi * im).astype(BF16)
            grads[at, part, 1] = (pr * im - pi * re).astype(BF16)
            adjoint[0, sides[part]] = tr * re + ti * im
            adjoint[1, sides[part]] = tr * im - ti * re

        @pl.when(at != depth)
        def _():
            for copy in grad_near(at):
                copy.start()

        return carry

    lax.fori_loop(0, n_depth, backward, 0)

    @pl.when(depth != 0)
    def _():
        for copy in grad_near(0):
            copy.wait_send()

    for at in range(n_depth):

        @pl.when(at != depth)
        def _(at=at):
            grad_far(at).start()

    for part in range(2):
        for plane in range(2):
            came[depth, part, plane] = grads[depth, part, plane]
    zero = jnp.zeros((rows // 2, width), BF16)
    strip_copies = []
    for number, (plane, span) in enumerate(chunks):
        for offset in range(n_depth - 1):
            send(grads.at[0, 0, plane, span], came.at[0, 0, plane, span], ga_s.at[offset, number],
                 ga_r.at[offset, number], (depth, scan)).wait_recv()
        for piece in range(2):
            start = span.start + piece * (rows // 2)
            at_rows = slice(start, start + rows // 2)
            lows, highs = [], []
            for slot in range(slots):
                value = came[slot, 0, plane, at_rows]
                is_low = low[slot, at_rows] > 0.5
                lows.append(jnp.where(is_low, value, zero))
                highs.append(jnp.where(is_low, zero, value))
            for at in range(blocks):
                for target, values in ((strip_low, lows), (strip_high, highs)):
                    terms = [
                        jnp.where(blk[slot, : rows // 2] == at, values[slot], zero)
                        for slot in range(slots)
                    ]
                    total = (terms[0] + terms[1]) + (terms[2] + terms[3])
                    target[plane, at_rows, columns(at)] = total
        pair = [
            send(strip_low.at[plane, span], got_low.at[plane, span], strip_s.at[0, number],
                 strip_r.at[0, number], (depth, before)),
            send(strip_high.at[plane, span], got_high.at[plane, span], strip_s.at[1, number],
                 strip_r.at[1, number], (depth, after)),
        ]
        for copy in pair:
            copy.start()
        strip_copies.append(pair)

    for offset in range(n_depth - 1):
        send(grads.at[0, 1], came.at[0, 1], gb_s.at[offset], gb_r.at[offset],
             (depth, scan)).wait_recv()
    for plane in range(2):
        for piece in range(4):
            at_rows = slice(piece * (rows // 2), (piece + 1) * (rows // 2))
            values = [came[slot, 1, plane, at_rows] for slot in range(slots)]
            for at in range(blocks):
                terms = [
                    jnp.where(blk[slot, : rows // 2] == at, values[slot], zero).astype(F32)
                    for slot in range(slots)
                ]
                total = (terms[0] + terms[1]) + (terms[2] + terms[3])
                out_ref[0, plane, at_rows, columns(at)] = total
    for number, (plane, span) in enumerate(chunks):
        for copy in strip_copies[number]:
            copy.wait_recv()
        out_ref[0, plane, span] = out_ref[0, plane, span] + (
            got_low[plane, span].astype(F32) + got_high[plane, span].astype(F32)
        )

    par_copy.wait_send()
    meas_copy.wait_send()
    for copy in b_copies + a_copies:
        copy.wait_send()
    for pair in tile_copies + strip_copies:
        for copy in pair:
            copy.wait_send()
    for step in range(1, n_depth):
        at = lax.rem(depth + step, n_depth)
        grad_far(at).wait_send()

        @pl.when(at != 0)
        def _(at=at):
            for copy in grad_near(at):
                copy.wait_send()


def body(transmission, probe_wave, prop_phase, measured, scan_rows, scan_cols, live_counts):
    width = probe_wave.shape[-1]
    half = transmission.shape[2]
    columns = transmission.shape[3]
    n_depth = lax.axis_size("depth")
    t1, t2 = dft_blocks(width)
    dma = pltpu.SemaphoreType.DMA
    others = n_depth - 1
    scratch = [
        pltpu.SMEM((n_depth,), jnp.int32),
        pltpu.SMEM((n_depth,), jnp.int32),
        pltpu.SMEM((1,), jnp.int32),
        pltpu.VMEM((n_depth, half // 2, width), BF16),
        pltpu.VMEM((n_depth, half, width), BF16),
        pltpu.VMEM((2, half, columns), F32),
        pltpu.VMEM((2, half, columns), BF16),
        pltpu.VMEM((2, width, width), F32),
        pltpu.VMEM((width, width), F32),
        pltpu.VMEM((width, width), F32),
        pltpu.VMEM((width, width), F32),
        pltpu.VMEM((width, width), F32),
        pltpu.VMEM((2, width, width), BF16),
        pltpu.VMEM((2, width, width), BF16),
        pltpu.VMEM((16, width), jnp.int32),
        pltpu.VMEM((16, width), jnp.int32),
        pltpu.VMEM((2, half, columns), BF16),
        pltpu.VMEM((2, half, columns), BF16),
        pltpu.VMEM((others, 2, half, width), BF16),
        pltpu.VMEM((others, 2, half, width), BF16),
        pltpu.VMEM((n_depth, 2, 2, half, width), BF16),
        pltpu.VMEM((2, width, width), F32),
        pltpu.VMEM((n_depth + 1, 2, width, width), BF16),
        pltpu.VMEM((2, width, width), F32),
        pltpu.VMEM((2, width, width), BF16),
        pltpu.VMEM((2, width, width), BF16),
        pltpu.VMEM((n_depth, 2, 2, half, width), BF16),
        pltpu.VMEM((n_depth, 2, 2, half, width), BF16),
        pltpu.VMEM((2, half, columns), BF16),
        pltpu.VMEM((2, half, columns), BF16),
        pltpu.VMEM((2, half, columns), BF16),
        pltpu.VMEM((2, half, columns), BF16),
        dma((10,)),
        dma((2,)),
        dma((2, 4)),
        dma((2, 4)),
        dma((2,)),
        dma((others,)),
        dma((others,)),
        dma((others, 4)),
        dma((others, 4)),
        dma((others,)),
        dma((others,)),
        dma((others, 4)),
        dma((others, 4)),
        dma((2, 4)),
        dma((2, 4)),
    ]
    anywhere = pl.BlockSpec(memory_space=pltpu.HBM)
    return pl.pallas_call(
        kernel,
        out_shape=pltpu.VMEM(transmission.shape, F32),
        in_specs=[anywhere] * 9,
        out_specs=pl.BlockSpec(memory_space=pltpu.VMEM),
        scratch_shapes=scratch,
        compiler_params=pltpu.CompilerParams(
            collective_id=0, has_side_effects=True, vmem_limit_bytes=57_000_000
        ),
    )(transmission, probe_wave, prop_phase, measured, scan_rows, scan_cols, live_counts, t1, t2)


def solution(mesh):
    in_specs = (
        P("depth", None, "scan", None),
        P(),
        P(),
        P("scan", None, None),
        P("scan"),
        P("scan"),
        P("scan"),
    )
    out_specs = P("depth", None, "scan", None)
    return jax.shard_map(body, mesh=mesh, in_specs=in_specs, out_specs=out_specs, check_vma=False)
```

```python
import functools
import math

import jax
import jax.numpy as jnp
import numpy as np
from jax import lax
from jax.experimental import pallas as pl
from jax.experimental.pallas import tpu as pltpu
from jax.sharding import PartitionSpec as P

MESH = pl.DeviceIdType.MESH
BF16 = jnp.bfloat16
F32 = jnp.float32


def dft_blocks(pixels):
    index = np.arange(pixels)
    angles = (index[:, None] * index[None, :] % pixels) * (2.0 * math.pi / pixels)
    scale = 1.0 / math.sqrt(pixels)
    re, im = np.cos(angles) * scale, -np.sin(angles) * scale
    blocks = []
    for parity in range(2):
        r, i = re[parity::2, : pixels // 2], im[parity::2, : pixels // 2]
        blocks.append(np.block([[r, -i], [i, r]]))
    blocks = np.stack(blocks)
    return jnp.asarray(blocks, F32).astype(BF16), jnp.asarray(blocks.swapaxes(1, 2), F32).astype(BF16)


def kernel(
    tile_hbm, probe_hbm, phase_hbm, meas_hbm, rows_hbm, cols_hbm, live_hbm, t1_hbm, t2_hbm,
    out_ref,
    rows_s, cols_s, live_s, blk, low, tile32, tile16, probe32, phase, meas_in, meas_out, meas, t1, t2, par_out, par_in,
    lower, upper, crops_b, crops_a, patch, prop, psi, adjoint, xs, us, grads, came,
    strip_low, strip_high, got_low, got_high,
    load_sem, par_sem, tile_sem_s, tile_sem_r, meas_sem,
    bx_s, bx_r, ax_s, ax_r, gb_s, gb_r, ga_s, ga_r, strip_s, strip_r,
):
    depth = lax.axis_index("depth")
    scan = lax.axis_index("scan")
    n_depth = lax.axis_size("depth")
    n_scan = lax.axis_size("scan")
    after = lax.rem(scan + 1, n_scan)
    before = lax.rem(scan + n_scan - 1, n_scan)
    half, width = patch.shape[3], patch.shape[4]
    blocks = tile32.shape[2] // width
    slots = n_depth
    rows = half // 2
    chunks = [(plane, slice(part * rows, (part + 1) * rows)) for plane in range(2) for part in range(2)]

    def peer(offset):
        return (lax.rem(depth + offset, n_depth), scan)

    loads = [
        pltpu.make_async_copy(tile_hbm.at[0, 0], tile32.at[0], load_sem.at[0]),
        pltpu.make_async_copy(tile_hbm.at[0, 1], tile32.at[1], load_sem.at[1]),
        pltpu.make_async_copy(probe_hbm, probe32, load_sem.at[2]),
        pltpu.make_async_copy(phase_hbm, phase, load_sem.at[3]),
        pltpu.make_async_copy(t1_hbm, t1, load_sem.at[4]),
        pltpu.make_async_copy(t2_hbm, t2, load_sem.at[5]),
        pltpu.make_async_copy(rows_hbm, rows_s, load_sem.at[6]),
        pltpu.make_async_copy(cols_hbm, cols_s, load_sem.at[7]),
        pltpu.make_async_copy(live_hbm, live_s, load_sem.at[8]),
        pltpu.make_async_copy(meas_hbm.at[depth], meas_in, load_sem.at[9]),
    ]
    for at in (6, 7, 8, 0, 1, 9, 3, 2, 4, 5):
        loads[at].start()

    barrier = pltpu.get_barrier_semaphore()
    for offset in range(1, n_depth):
        pl.semaphore_signal(barrier, inc=1, device_id=peer(offset), device_id_type=MESH)
    pl.semaphore_signal(barrier, inc=1, device_id=(depth, after), device_id_type=MESH)
    pl.semaphore_signal(barrier, inc=1, device_id=(depth, before), device_id_type=MESH)
    for load in loads[6:9]:
        load.wait()
    for slot in range(slots):
        par_out[slot : slot + 1, :] = jnp.full((1, width), rows_s[slot], jnp.int32)
        par_out[slots + slot : slots + slot + 1, :] = jnp.full((1, width), cols_s[slot], jnp.int32)
    par_out[2 * slots : 2 * slots + 1, :] = jnp.full((1, width), live_s[0], jnp.int32)
    pl.semaphore_wait(barrier, n_depth + 1)

    def send(src, dst, s_sem, r_sem, device):
        return pltpu.make_async_remote_copy(
            src_ref=src, dst_ref=dst, send_sem=s_sem, recv_sem=r_sem,
            device_id=device, device_id_type=MESH,
        )

    par_copy = send(par_out, par_in, par_sem.at[0], par_sem.at[1], (depth, after))
    par_copy.start()
    tile_copies = []
    for at, (plane, span) in enumerate(chunks):
        if at % 2 == 0:
            loads[plane].wait()
        tile16[plane, span] = tile32[plane, span].astype(BF16)
        pair = [
            send(tile16.at[plane, span], lower.at[plane, span], tile_sem_s.at[0, at],
                 tile_sem_r.at[0, at], (depth, after)),
            send(tile16.at[plane, span], upper.at[plane, span], tile_sem_s.at[1, at],
                 tile_sem_r.at[1, at], (depth, before)),
        ]
        for copy in pair:
            copy.start()
        tile_copies.append(pair)
    par_copy.wait_recv()
    row_at = lax.broadcasted_iota(jnp.int32, (half, width), 0)
    lane_at = lax.broadcasted_iota(jnp.int32, (rows, width), 1)
    for slot in range(slots):
        first = jnp.broadcast_to(par_in[slots + slot : slots + slot + 1, :], (rows, width))
        block = (first >> 8) + jnp.where(lane_at < (first & (width - 1)), 1, 0)
        blk[slot] = block.astype(F32).astype(BF16)
        begin = jnp.broadcast_to(par_in[slot : slot + 1, :], (half, width))
        low[slot] = jnp.where(row_at >= begin, 1.0, 0.0).astype(BF16)

    def pick(slot, values):
        piece = values[0]
        for at in range(1, blocks):
            piece = jnp.where(blk[slot] == at, values[at], piece)
        return piece

    def columns(at):
        return slice(at * width, (at + 1) * width)

    b_copies = []
    for offset in (*range(1, n_depth), 0):
        slot = lax.rem(depth + offset, n_depth)
        for plane, span in chunks:
            piece = pick(slot, [tile16[plane, span, columns(at)] for at in range(blocks)])
            if offset == 0:
                patch[depth, 1, plane, span] = piece
            else:
                crops_b[offset - 1, plane, span] = piece
        if offset:
            copy = send(crops_b.at[offset - 1], patch.at[depth, 1], bx_s.at[offset - 1],
                        bx_r.at[offset - 1], peer(offset))
            copy.start()
            b_copies.append(copy)

    big_row = lax.broadcasted_iota(jnp.int32, (width, width), 0)
    big_lane = lax.broadcasted_iota(jnp.int32, (width, width), 1)
    to_split = jnp.where(2 * (big_row & (half - 1)) + (big_row // half) == big_lane, 1.0, 0.0).astype(BF16)
    of_split = jnp.where(2 * (big_lane & (half - 1)) + (big_lane // half) == big_row, 1.0, 0.0).astype(BF16)

    def split_order(value, parts):
        total = jnp.zeros_like(value)
        for _ in range(parts):
            part = value.astype(BF16)
            value = value - part.astype(F32)
            moved = jnp.dot(to_split, part, preferred_element_type=F32).astype(BF16)
            total = total + jnp.dot(moved, of_split, preferred_element_type=F32)
        return total

    loads[9].wait()
    meas_out[...] = split_order(meas_in[...], 3)
    meas_copy = send(meas_out, meas, meas_sem.at[0], meas_sem.at[1], (depth, after))
    meas_copy.start()
    loads[3].wait()
    phase[...] = split_order(phase[...], 3)
    prop[0] = jnp.cos(phase[...])

    loads[2].wait()
    own_row = jnp.broadcast_to(par_in[pl.ds(depth, 1), :], (width, width))
    own_col = jnp.broadcast_to(par_in[pl.ds(slots + depth, 1), :], (width, width))
    down = jnp.where(((big_row - own_row) & (width - 1)) == big_lane, 1.0, 0.0).astype(BF16)
    across = jnp.where(((big_row + own_col) & (width - 1)) == big_lane, 1.0, 0.0).astype(BF16)
    for plane in range(2):
        rolled = jnp.dot(down, probe32[plane].astype(BF16), preferred_element_type=F32)
        rolled = jnp.dot(rolled.astype(BF16), across, preferred_element_type=F32)
        psi[0, plane] = rolled.astype(BF16)

    a_copies = []
    for number, (plane, span) in enumerate(chunks):
        for copy in tile_copies[number]:
            copy.wait_recv()
        for offset in (*range(1, n_depth), 0):
            slot = lax.rem(depth + offset, n_depth)
            is_low = low[slot, span] > 0.5
            piece = pick(slot, [
                jnp.where(is_low, lower[plane, span, columns(at)], upper[plane, span, columns(at)])
                for at in range(blocks)
            ])
            if offset == 0:
                patch[depth, 0, plane, span] = piece
            else:
                crops_a[offset - 1, plane, span] = piece
                copy = send(crops_a.at[offset - 1, plane, span], patch.at[depth, 0, plane, span],
                            ax_s.at[offset - 1, number], ax_r.at[offset - 1, number],
                            peer(offset))
                copy.start()
                a_copies.append(copy)

    prop[1] = jnp.sin(phase[...])
    loads[4].wait()
    loads[5].wait()
    sides = [slice(0, half), slice(half, width)]

    def to_frequencies(upper_re, upper_im, lower_re, lower_im):
        xs[0, :half] = (upper_re + lower_re).astype(BF16)
        xs[0, half:] = (upper_im + lower_im).astype(BF16)
        xs[1, :half] = (upper_re - lower_re).astype(BF16)
        xs[1, half:] = (upper_im - lower_im).astype(BF16)
        for parity in range(2):
            inner = jnp.dot(t1[parity], xs[parity], preferred_element_type=F32)
            for part in range(2):
                left, right = inner[sides[part], :half], inner[sides[part], half:]
                us[0, sides[parity], sides[part]] = (left + right).astype(BF16)
                us[1, sides[parity], sides[part]] = (left - right).astype(BF16)
        return [
            jnp.dot(us[parity], t2[parity], preferred_element_type=F32) for parity in range(2)
        ]

    def keep(parity, re, im):
        for part in range(2):
            xs[part, :half, sides[parity]] = re[sides[part]].astype(BF16)
            xs[part, half:, sides[parity]] = im[sides[part]].astype(BF16)

    def to_positions():
        even = jnp.dot(t2[0], xs[0], preferred_element_type=F32)
        odd = jnp.dot(t2[1], xs[1], preferred_element_type=F32)
        for part in range(2):
            upper_half = (even[sides[part]] + odd[sides[part]]).astype(BF16)
            lower_half = (even[sides[part]] - odd[sides[part]]).astype(BF16)
            for parity in range(2):
                us[parity, :half, sides[part]] = upper_half[:, sides[parity]]
                us[parity, half:, sides[part]] = lower_half[:, sides[parity]]
        even = jnp.dot(us[0], t1[0], preferred_element_type=F32)
        odd = jnp.dot(us[1], t1[1], preferred_element_type=F32)
        return [
            jnp.concatenate([even[:, side] + odd[:, side], even[:, side] - odd[:, side]], axis=1)
            for side in sides
        ]

    def propagate(halves, sign):
        both = to_frequencies(*halves)
        for parity in range(2):
            re, im = both[parity][:, :half], both[parity][:, half:]
            pr, pi = prop[0, :, sides[parity]], sign * prop[1, :, sides[parity]]
            keep(parity, re * pr - im * pi, re * pi + im * pr)
        return to_positions()

    def forward(at, carry):
        @pl.when(at != depth)
        def _():
            offset = lax.rem(depth + n_depth - at, n_depth) - 1
            send(crops_b.at[offset], patch.at[at, 1], bx_s.at[offset], bx_r.at[offset],
                 (at, scan)).wait_recv()
            for number, (plane, rows_at) in enumerate(chunks):
                send(crops_a.at[offset, plane, rows_at], patch.at[at, 0, plane, rows_at],
                     ax_s.at[offset, number], ax_r.at[offset, number],
                     (at, scan)).wait_recv()

        halves = []
        for part in range(2):
            tr, ti = patch[at, part, 0].astype(F32), patch[at, part, 1].astype(F32)
            pr, pi = psi[at, 0, sides[part]].astype(F32), psi[at, 1, sides[part]].astype(F32)
            halves += [tr * pr - ti * pi, tr * pi + ti * pr]
        re, im = propagate(halves, 1.0)
        psi[at + 1, 0] = re.astype(BF16)
        psi[at + 1, 1] = im.astype(BF16)
        return carry

    lax.fori_loop(0, n_depth, forward, 0)

    leaving = [psi[n_depth, plane, side].astype(F32) for side in sides for plane in range(2)]
    both = to_frequencies(*leaving)
    meas_copy.wait_recv()
    live = jnp.where(
        jnp.broadcast_to(par_in[2 * slots : 2 * slots + 1, :half], (width, half)) > depth, 1.0, 0.0
    )
    for parity in range(2):
        re, im = both[parity][:, :half], both[parity][:, half:]
        factor = live * (1.0 - meas[:, sides[parity]] / jnp.sqrt(re * re + im * im + 1.0))
        keep(parity, factor * re, factor * im)
    re, im = to_positions()
    adjoint[0] = re
    adjoint[1] = im

    def grad_near(at):
        offset = lax.rem(at + n_depth - depth, n_depth) - 1
        return [
            send(grads.at[at, 0, plane, span], came.at[depth, 0, plane, span],
                 ga_s.at[offset, number], ga_r.at[offset, number], (at, scan))
            for number, (plane, span) in enumerate(chunks)
        ]

    def grad_far(at):
        offset = lax.rem(at + n_depth - depth, n_depth) - 1
        return send(grads.at[at, 1], came.at[depth, 1], gb_s.at[offset], gb_r.at[offset],
                    (at, scan))

    def backward(step, carry):
        at = n_depth - 1 - step
        mu_re, mu_im = propagate([adjoint[plane, side] for side in sides for plane in range(2)], -1.0)
        for part in range(2):
            re, im = mu_re[sides[part]], mu_im[sides[part]]
            tr, ti = patch[at, part, 0].astype(F32), patch[at, part, 1].astype(F32)
            pr, pi = psi[at, 0, sides[part]].astype(F32), psi[at, 1, sides[part]].astype(F32)
            grads[at, part, 0] = (pr * re + pi * im).astype(BF16)
            grads[at, part, 1] = (pr * im - pi * re).astype(BF16)
            adjoint[0, sides[part]] = tr * re + ti * im
            adjoint[1, sides[part]] = tr * im - ti * re

        @pl.when(at != depth)
        def _():
            for copy in grad_near(at):
                copy.start()

        return carry

    lax.fori_loop(0, n_depth, backward, 0)

    for back in range(n_depth):
        at = n_depth - 1 - back

        @pl.when(at != depth)
        def _(at=at):
            grad_far(at).start()

    for part in range(2):
        for plane in range(2):
            came[depth, part, plane] = grads[depth, part, plane]
    zero = jnp.zeros((rows // 2, width), BF16)
    strip_copies = []
    for number, (plane, span) in enumerate(chunks):
        for offset in range(n_depth - 1):
            send(grads.at[0, 0, plane, span], came.at[0, 0, plane, span], ga_s.at[offset, number],
                 ga_r.at[offset, number], (depth, scan)).wait_recv()
        for piece in range(2):
            start = span.start + piece * (rows // 2)
            at_rows = slice(start, start + rows // 2)
            lows, highs = [], []
            for slot in range(slots):
                value = came[slot, 0, plane, at_rows]
                is_low = low[slot, at_rows] > 0.5
                lows.append(jnp.where(is_low, value, zero))
                highs.append(jnp.where(is_low, zero, value))
            for at in range(blocks):
                for target, values in ((strip_low, lows), (strip_high, highs)):
                    terms = [
                        jnp.where(blk[slot, : rows // 2] == at, values[slot], zero)
                        for slot in range(slots)
                    ]
                    total = (terms[0] + terms[1]) + (terms[2] + terms[3])
                    target[plane, at_rows, columns(at)] = total
        pair = [
            send(strip_low.at[plane, span], got_low.at[plane, span], strip_s.at[0, number],
                 strip_r.at[0, number], (depth, before)),
            send(strip_high.at[plane, span], got_high.at[plane, span], strip_s.at[1, number],
                 strip_r.at[1, number], (depth, after)),
        ]
        for copy in pair:
            copy.start()
        strip_copies.append(pair)

    for offset in range(n_depth - 1):
        send(grads.at[0, 1], came.at[0, 1], gb_s.at[offset], gb_r.at[offset],
             (depth, scan)).wait_recv()
    for plane in range(2):
        for piece in range(4):
            at_rows = slice(piece * (rows // 2), (piece + 1) * (rows // 2))
            values = [came[slot, 1, plane, at_rows] for slot in range(slots)]
            for at in range(blocks):
                terms = [
                    jnp.where(blk[slot, : rows // 2] == at, values[slot], zero).astype(F32)
                    for slot in range(slots)
                ]
                total = (terms[0] + terms[1]) + (terms[2] + terms[3])
                out_ref[0, plane, at_rows, columns(at)] = total
    for number, (plane, span) in enumerate(chunks):
        for copy in strip_copies[number]:
            copy.wait_recv()
        out_ref[0, plane, span] = out_ref[0, plane, span] + (
            got_low[plane, span].astype(F32) + got_high[plane, span].astype(F32)
        )

    par_copy.wait_send()
    meas_copy.wait_send()
    for copy in b_copies + a_copies:
        copy.wait_send()
    for pair in tile_copies + strip_copies:
        for copy in pair:
            copy.wait_send()
    for step in range(1, n_depth):
        at = lax.rem(depth + step, n_depth)
        for copy in grad_near(at) + [grad_far(at)]:
            copy.wait_send()


def body(transmission, probe_wave, prop_phase, measured, scan_rows, scan_cols, live_counts):
    width = probe_wave.shape[-1]
    half = transmission.shape[2]
    columns = transmission.shape[3]
    n_depth = lax.axis_size("depth")
    t1, t2 = dft_blocks(width)
    dma = pltpu.SemaphoreType.DMA
    others = n_depth - 1
    scratch = [
        pltpu.SMEM((n_depth,), jnp.int32),
        pltpu.SMEM((n_depth,), jnp.int32),
        pltpu.SMEM((1,), jnp.int32),
        pltpu.VMEM((n_depth, half // 2, width), BF16),
        pltpu.VMEM((n_depth, half, width), BF16),
        pltpu.VMEM((2, half, columns), F32),
        pltpu.VMEM((2, half, columns), BF16),
        pltpu.VMEM((2, width, width), F32),
        pltpu.VMEM((width, width), F32),
        pltpu.VMEM((width, width), F32),
        pltpu.VMEM((width, width), F32),
        pltpu.VMEM((width, width), F32),
        pltpu.VMEM((2, width, width), BF16),
        pltpu.VMEM((2, width, width), BF16),
        pltpu.VMEM((16, width), jnp.int32),
        pltpu.VMEM((16, width), jnp.int32),
        pltpu.VMEM((2, half, columns), BF16),
        pltpu.VMEM((2, half, columns), BF16),
        pltpu.VMEM((others, 2, half, width), BF16),
        pltpu.VMEM((others, 2, half, width), BF16),
        pltpu.VMEM((n_depth, 2, 2, half, width), BF16),
        pltpu.VMEM((2, width, width), F32),
        pltpu.VMEM((n_depth + 1, 2, width, width), BF16),
        pltpu.VMEM((2, width, width), F32),
        pltpu.VMEM((2, width, width), BF16),
        pltpu.VMEM((2, width, width), BF16),
        pltpu.VMEM((n_depth, 2, 2, half, width), BF16),
        pltpu.VMEM((n_depth, 2, 2, half, width), BF16),
        pltpu.VMEM((2, half, columns), BF16),
        pltpu.VMEM((2, half, columns), BF16),
        pltpu.VMEM((2, half, columns), BF16),
        pltpu.VMEM((2, half, columns), BF16),
        dma((10,)),
        dma((2,)),
        dma((2, 4)),
        dma((2, 4)),
        dma((2,)),
        dma((others,)),
        dma((others,)),
        dma((others, 4)),
        dma((others, 4)),
        dma((others,)),
        dma((others,)),
        dma((others, 4)),
        dma((others, 4)),
        dma((2, 4)),
        dma((2, 4)),
    ]
    anywhere = pl.BlockSpec(memory_space=pltpu.HBM)
    return pl.pallas_call(
        kernel,
        out_shape=pltpu.VMEM(transmission.shape, F32),
        in_specs=[anywhere] * 9,
        out_specs=pl.BlockSpec(memory_space=pltpu.VMEM),
        scratch_shapes=scratch,
        compiler_params=pltpu.CompilerParams(
            collective_id=0, has_side_effects=True, vmem_limit_bytes=57_000_000
        ),
    )(transmission, probe_wave, prop_phase, measured, scan_rows, scan_cols, live_counts, t1, t2)


def solution(mesh):
    in_specs = (
        P("depth", None, "scan", None),
        P(),
        P(),
        P("scan", None, None),
        P("scan"),
        P("scan"),
        P("scan"),
    )
    out_specs = P("depth", None, "scan", None)
    return jax.shard_map(body, mesh=mesh, in_specs=in_specs, out_specs=out_specs, check_vma=False)
```

```python
import functools
import math

import jax
import jax.numpy as jnp
import numpy as np
from jax import lax
from jax.experimental import pallas as pl
from jax.experimental.pallas import tpu as pltpu
from jax.sharding import PartitionSpec as P

MESH = pl.DeviceIdType.MESH
BF16 = jnp.bfloat16
F32 = jnp.float32


def dft_blocks(pixels):
    index = np.arange(pixels)
    angles = (index[:, None] * index[None, :] % pixels) * (2.0 * math.pi / pixels)
    scale = 1.0 / math.sqrt(pixels)
    re, im = np.cos(angles) * scale, -np.sin(angles) * scale
    blocks = []
    for parity in range(2):
        r, i = re[parity::2, : pixels // 2], im[parity::2, : pixels // 2]
        blocks.append(np.block([[r, -i], [i, r]]))
    blocks = np.stack(blocks)
    return jnp.asarray(blocks, F32).astype(BF16), jnp.asarray(blocks.swapaxes(1, 2), F32).astype(BF16)


def kernel(
    tile_hbm, probe_hbm, phase_hbm, meas_hbm, rows_hbm, cols_hbm, live_hbm, t1_hbm, t2_hbm,
    out_ref,
    rows_s, cols_s, live_s, blk, low, tile32, tile16, probe32, phase, meas_in, meas_out, meas, t1, t2, par_out, par_in,
    lower, upper, crops_b, crops_a, patch, prop, psi, adjoint, xs, us, grads, came,
    strip_low, strip_high, got_low, got_high,
    load_sem, par_sem, tile_sem_s, tile_sem_r, meas_sem,
    bx_s, bx_r, ax_s, ax_r, gb_s, gb_r, ga_s, ga_r, strip_s, strip_r,
):
    depth = lax.axis_index("depth")
    scan = lax.axis_index("scan")
    n_depth = lax.axis_size("depth")
    n_scan = lax.axis_size("scan")
    after = lax.rem(scan + 1, n_scan)
    before = lax.rem(scan + n_scan - 1, n_scan)
    half, width = patch.shape[3], patch.shape[4]
    blocks = tile32.shape[2] // width
    slots = n_depth
    rows = half // 2
    order = (n_depth // 2, *(at for at in range(1, n_depth) if at != n_depth // 2), 0)
    chunks = [(plane, slice(part * rows, (part + 1) * rows)) for plane in range(2) for part in range(2)]

    def peer(offset):
        return (lax.rem(depth + offset, n_depth), scan)

    barrier = pltpu.get_barrier_semaphore()
    for offset in range(1, n_depth):
        pl.semaphore_signal(barrier, inc=1, device_id=peer(offset), device_id_type=MESH)
    pl.semaphore_signal(barrier, inc=1, device_id=(depth, after), device_id_type=MESH)
    pl.semaphore_signal(barrier, inc=1, device_id=(depth, before), device_id_type=MESH)
    loads = [
        pltpu.make_async_copy(tile_hbm.at[0, 0], tile32.at[0], load_sem.at[0]),
        pltpu.make_async_copy(tile_hbm.at[0, 1], tile32.at[1], load_sem.at[1]),
        pltpu.make_async_copy(probe_hbm, probe32, load_sem.at[2]),
        pltpu.make_async_copy(phase_hbm, phase, load_sem.at[3]),
        pltpu.make_async_copy(t1_hbm, t1, load_sem.at[4]),
        pltpu.make_async_copy(t2_hbm, t2, load_sem.at[5]),
        pltpu.make_async_copy(rows_hbm, rows_s, load_sem.at[6]),
        pltpu.make_async_copy(cols_hbm, cols_s, load_sem.at[7]),
        pltpu.make_async_copy(live_hbm, live_s, load_sem.at[8]),
        pltpu.make_async_copy(meas_hbm.at[depth], meas_in, load_sem.at[9]),
    ]
    for at in (6, 7, 8, 0, 1, 9, 3, 2, 4, 5):
        loads[at].start()

    for load in loads[6:9]:
        load.wait()
    for slot in range(slots):
        par_out[slot : slot + 1, :] = jnp.full((1, width), rows_s[slot], jnp.int32)
        par_out[slots + slot : slots + slot + 1, :] = jnp.full((1, width), cols_s[slot], jnp.int32)
    par_out[2 * slots : 2 * slots + 1, :] = jnp.full((1, width), live_s[0], jnp.int32)
    pl.semaphore_wait(barrier, n_depth + 1)

    def send(src, dst, s_sem, r_sem, device):
        return pltpu.make_async_remote_copy(
            src_ref=src, dst_ref=dst, send_sem=s_sem, recv_sem=r_sem,
            device_id=device, device_id_type=MESH,
        )

    par_copy = send(par_out, par_in, par_sem.at[0], par_sem.at[1], (depth, after))
    par_copy.start()
    tile_copies = []
    for at, (plane, span) in enumerate(chunks):
        if at % 2 == 0:
            loads[plane].wait()
        tile16[plane, span] = tile32[plane, span].astype(BF16)
        pair = [
            send(tile16.at[plane, span], lower.at[plane, span], tile_sem_s.at[0, at],
                 tile_sem_r.at[0, at], (depth, after)),
            send(tile16.at[plane, span], upper.at[plane, span], tile_sem_s.at[1, at],
                 tile_sem_r.at[1, at], (depth, before)),
        ]
        for copy in pair:
            copy.start()
        tile_copies.append(pair)
    par_copy.wait_recv()
    row_at = lax.broadcasted_iota(jnp.int32, (half, width), 0)
    lane_at = lax.broadcasted_iota(jnp.int32, (rows, width), 1)
    for slot in range(slots):
        first = jnp.broadcast_to(par_in[slots + slot : slots + slot + 1, :], (rows, width))
        block = (first >> 8) + jnp.where(lane_at < (first & (width - 1)), 1, 0)
        blk[slot] = block.astype(F32).astype(BF16)

    def pick(slot, values):
        piece = values[0]
        for at in range(1, blocks):
            piece = jnp.where(blk[slot] == at, values[at], piece)
        return piece

    def columns(at):
        return slice(at * width, (at + 1) * width)

    b_copies = []
    for offset in order:
        slot = lax.rem(depth + offset, n_depth)
        for plane, span in chunks:
            piece = pick(slot, [tile16[plane, span, columns(at)] for at in range(blocks)])
            if offset == 0:
                patch[depth, 1, plane, span] = piece
            else:
                crops_b[offset - 1, plane, span] = piece
        if offset:
            copy = send(crops_b.at[offset - 1], patch.at[depth, 1], bx_s.at[offset - 1],
                        bx_r.at[offset - 1], peer(offset))
            copy.start()
            b_copies.append(copy)

    for slot in range(slots):
        begin = jnp.broadcast_to(par_in[slot : slot + 1, :], (half, width))
        low[slot] = jnp.where(row_at >= begin, 1.0, 0.0).astype(BF16)

    big_row = lax.broadcasted_iota(jnp.int32, (width, width), 0)
    big_lane = lax.broadcasted_iota(jnp.int32, (width, width), 1)
    to_split = jnp.where(2 * (big_row & (half - 1)) + (big_row // half) == big_lane, 1.0, 0.0).astype(BF16)
    of_split = jnp.where(2 * (big_lane & (half - 1)) + (big_lane // half) == big_row, 1.0, 0.0).astype(BF16)

    def split_order(value, parts):
        total = jnp.zeros_like(value)
        for _ in range(parts):
            part = value.astype(BF16)
            value = value - part.astype(F32)
            moved = jnp.dot(to_split, part, preferred_element_type=F32).astype(BF16)
            total = total + jnp.dot(moved, of_split, preferred_element_type=F32)
        return total

    loads[9].wait()
    meas_out[...] = split_order(meas_in[...], 3)
    meas_copy = send(meas_out, meas, meas_sem.at[0], meas_sem.at[1], (depth, after))
    meas_copy.start()
    loads[3].wait()
    phase[...] = split_order(phase[...], 3)
    prop[0] = jnp.cos(phase[...])

    loads[2].wait()
    own_row = jnp.broadcast_to(par_in[pl.ds(depth, 1), :], (width, width))
    own_col = jnp.broadcast_to(par_in[pl.ds(slots + depth, 1), :], (width, width))
    down = jnp.where(((big_row - own_row) & (width - 1)) == big_lane, 1.0, 0.0).astype(BF16)
    across = jnp.where(((big_row + own_col) & (width - 1)) == big_lane, 1.0, 0.0).astype(BF16)
    for plane in range(2):
        rolled = jnp.dot(down, probe32[plane].astype(BF16), preferred_element_type=F32)
        rolled = jnp.dot(rolled.astype(BF16), across, preferred_element_type=F32)
        psi[0, plane] = rolled.astype(BF16)

    a_copies = []
    for number, (plane, span) in enumerate(chunks):
        for copy in tile_copies[number]:
            copy.wait_recv()
        for offset in order:
            slot = lax.rem(depth + offset, n_depth)
            is_low = low[slot, span] > 0.5
            piece = pick(slot, [
                jnp.where(is_low, lower[plane, span, columns(at)], upper[plane, span, columns(at)])
                for at in range(blocks)
            ])
            if offset == 0:
                patch[depth, 0, plane, span] = piece
            else:
                crops_a[offset - 1, plane, span] = piece
                copy = send(crops_a.at[offset - 1, plane, span], patch.at[depth, 0, plane, span],
                            ax_s.at[offset - 1, number], ax_r.at[offset - 1, number],
                            peer(offset))
                copy.start()
                a_copies.append(copy)

    prop[1] = jnp.sin(phase[...])
    loads[4].wait()
    loads[5].wait()
    sides = [slice(0, half), slice(half, width)]

    def to_frequencies(upper_re, upper_im, lower_re, lower_im):
        xs[0, :half] = (upper_re + lower_re).astype(BF16)
        xs[0, half:] = (upper_im + lower_im).astype(BF16)
        xs[1, :half] = (upper_re - lower_re).astype(BF16)
        xs[1, half:] = (upper_im - lower_im).astype(BF16)
        for parity in range(2):
            inner = jnp.dot(t1[parity], xs[parity], preferred_element_type=F32)
            for part in range(2):
                left, right = inner[sides[part], :half], inner[sides[part], half:]
                us[0, sides[parity], sides[part]] = (left + right).astype(BF16)
                us[1, sides[parity], sides[part]] = (left - right).astype(BF16)
        return [
            jnp.dot(us[parity], t2[parity], preferred_element_type=F32) for parity in range(2)
        ]

    def keep(parity, re, im):
        for part in range(2):
            xs[part, :half, sides[parity]] = re[sides[part]].astype(BF16)
            xs[part, half:, sides[parity]] = im[sides[part]].astype(BF16)

    def to_positions():
        even = jnp.dot(t2[0], xs[0], preferred_element_type=F32)
        odd = jnp.dot(t2[1], xs[1], preferred_element_type=F32)
        for part in range(2):
            upper_half = (even[sides[part]] + odd[sides[part]]).astype(BF16)
            lower_half = (even[sides[part]] - odd[sides[part]]).astype(BF16)
            for parity in range(2):
                us[parity, :half, sides[part]] = upper_half[:, sides[parity]]
                us[parity, half:, sides[part]] = lower_half[:, sides[parity]]
        even = jnp.dot(us[0], t1[0], preferred_element_type=F32)
        odd = jnp.dot(us[1], t1[1], preferred_element_type=F32)
        return [
            jnp.concatenate([even[:, side] + odd[:, side], even[:, side] - odd[:, side]], axis=1)
            for side in sides
        ]

    def propagate(halves, sign):
        both = to_frequencies(*halves)
        for parity in range(2):
            re, im = both[parity][:, :half], both[parity][:, half:]
            pr, pi = prop[0, :, sides[parity]], sign * prop[1, :, sides[parity]]
            keep(parity, re * pr - im * pi, re * pi + im * pr)
        return to_positions()

    def forward(at, carry):
        @pl.when(at != depth)
        def _():
            offset = lax.rem(depth + n_depth - at, n_depth) - 1
            send(crops_b.at[offset], patch.at[at, 1], bx_s.at[offset], bx_r.at[offset],
                 (at, scan)).wait_recv()
            for number, (plane, rows_at) in enumerate(chunks):
                send(crops_a.at[offset, plane, rows_at], patch.at[at, 0, plane, rows_at],
                     ax_s.at[offset, number], ax_r.at[offset, number],
                     (at, scan)).wait_recv()

        halves = []
        for part in range(2):
            tr, ti = patch[at, part, 0].astype(F32), patch[at, part, 1].astype(F32)
            pr, pi = psi[at, 0, sides[part]].astype(F32), psi[at, 1, sides[part]].astype(F32)
            halves += [tr * pr - ti * pi, tr * pi + ti * pr]
        re, im = propagate(halves, 1.0)
        psi[at + 1, 0] = re.astype(BF16)
        psi[at + 1, 1] = im.astype(BF16)
        return carry

    lax.fori_loop(0, n_depth, forward, 0)

    leaving = [psi[n_depth, plane, side].astype(F32) for side in sides for plane in range(2)]
    both = to_frequencies(*leaving)
    meas_copy.wait_recv()
    live = jnp.where(
        jnp.broadcast_to(par_in[2 * slots : 2 * slots + 1, :half], (width, half)) > depth, 1.0, 0.0
    )
    for parity in range(2):
        re, im = both[parity][:, :half], both[parity][:, half:]
        factor = live * (1.0 - meas[:, sides[parity]] / jnp.sqrt(re * re + im * im + 1.0))
        keep(parity, factor * re, factor * im)
    re, im = to_positions()
    adjoint[0] = re
    adjoint[1] = im

    def grad_near(at):
        offset = lax.rem(at + n_depth - depth, n_depth) - 1
        return [
            send(grads.at[at, 0, plane, span], came.at[depth, 0, plane, span],
                 ga_s.at[offset, number], ga_r.at[offset, number], (at, scan))
            for number, (plane, span) in enumerate(chunks)
        ]

    def grad_far(at):
        offset = lax.rem(at + n_depth - depth, n_depth) - 1
        return send(grads.at[at, 1], came.at[depth, 1], gb_s.at[offset], gb_r.at[offset],
                    (at, scan))

    def backward(step, carry):
        at = n_depth - 1 - step
        mu_re, mu_im = propagate([adjoint[plane, side] for side in sides for plane in range(2)], -1.0)
        for part in range(2):
            re, im = mu_re[sides[part]], mu_im[sides[part]]
            tr, ti = patch[at, part, 0].astype(F32), patch[at, part, 1].astype(F32)
            pr, pi = psi[at, 0, sides[part]].astype(F32), psi[at, 1, sides[part]].astype(F32)
            grads[at, part, 0] = (pr * re + pi * im).astype(BF16)
            grads[at, part, 1] = (pr * im - pi * re).astype(BF16)
            adjoint[0, sides[part]] = tr * re + ti * im
            adjoint[1, sides[part]] = tr * im - ti * re
            if part == 0:

                @pl.when(at != depth)
                def _():
                    for copy in grad_near(at):
                        copy.start()

        return carry

    lax.fori_loop(0, n_depth, backward, 0)

    for back in range(n_depth):
        at = n_depth - 1 - back

        @pl.when(at != depth)
        def _(at=at):
            grad_far(at).start()

    for part in range(2):
        for plane in range(2):
            came[depth, part, plane] = grads[depth, part, plane]
    zero = jnp.zeros((rows // 2, width), BF16)
    strip_copies = []
    for number, (plane, span) in enumerate(chunks):
        for offset in range(n_depth - 1):
            send(grads.at[0, 0, plane, span], came.at[0, 0, plane, span], ga_s.at[offset, number],
                 ga_r.at[offset, number], (depth, scan)).wait_recv()
        for piece in range(2):
            start = span.start + piece * (rows // 2)
            at_rows = slice(start, start + rows // 2)
            lows, highs = [], []
            for slot in range(slots):
                value = came[slot, 0, plane, at_rows]
                is_low = low[slot, at_rows] > 0.5
                lows.append(jnp.where(is_low, value, zero))
                highs.append(jnp.where(is_low, zero, value))
            for at in range(blocks):
                for target, values in ((strip_low, lows), (strip_high, highs)):
                    terms = [
                        jnp.where(blk[slot, : rows // 2] == at, values[slot], zero)
                        for slot in range(slots)
                    ]
                    total = (terms[0] + terms[1]) + (terms[2] + terms[3])
                    target[plane, at_rows, columns(at)] = total
        pair = [
            send(strip_low.at[plane, span], got_low.at[plane, span], strip_s.at[0, number],
                 strip_r.at[0, number], (depth, before)),
            send(strip_high.at[plane, span], got_high.at[plane, span], strip_s.at[1, number],
                 strip_r.at[1, number], (depth, after)),
        ]
        for copy in pair:
            copy.start()
        strip_copies.append(pair)

    for offset in range(n_depth - 1):
        send(grads.at[0, 1], came.at[0, 1], gb_s.at[offset], gb_r.at[offset],
             (depth, scan)).wait_recv()
    for plane in range(2):
        for piece in range(4):
            at_rows = slice(piece * (rows // 2), (piece + 1) * (rows // 2))
            values = [came[slot, 1, plane, at_rows] for slot in range(slots)]
            for at in range(blocks):
                terms = [
                    jnp.where(blk[slot, : rows // 2] == at, values[slot], zero).astype(F32)
                    for slot in range(slots)
                ]
                total = (terms[0] + terms[1]) + (terms[2] + terms[3])
                out_ref[0, plane, at_rows, columns(at)] = total
    for number, (plane, span) in enumerate(chunks):
        for copy in strip_copies[number]:
            copy.wait_recv()
        out_ref[0, plane, span] = out_ref[0, plane, span] + (
            got_low[plane, span].astype(F32) + got_high[plane, span].astype(F32)
        )

    par_copy.wait_send()
    meas_copy.wait_send()
    for copy in b_copies + a_copies:
        copy.wait_send()
    for pair in tile_copies + strip_copies:
        for copy in pair:
            copy.wait_send()
    for step in range(1, n_depth):
        at = lax.rem(depth + step, n_depth)
        for copy in grad_near(at) + [grad_far(at)]:
            copy.wait_send()


def body(transmission, probe_wave, prop_phase, measured, scan_rows, scan_cols, live_counts):
    width = probe_wave.shape[-1]
    half = transmission.shape[2]
    columns = transmission.shape[3]
    n_depth = lax.axis_size("depth")
    t1, t2 = dft_blocks(width)
    dma = pltpu.SemaphoreType.DMA
    others = n_depth - 1
    scratch = [
        pltpu.SMEM((n_depth,), jnp.int32),
        pltpu.SMEM((n_depth,), jnp.int32),
        pltpu.SMEM((1,), jnp.int32),
        pltpu.VMEM((n_depth, half // 2, width), BF16),
        pltpu.VMEM((n_depth, half, width), BF16),
        pltpu.VMEM((2, half, columns), F32),
        pltpu.VMEM((2, half, columns), BF16),
        pltpu.VMEM((2, width, width), F32),
        pltpu.VMEM((width, width), F32),
        pltpu.VMEM((width, width), F32),
        pltpu.VMEM((width, width), F32),
        pltpu.VMEM((width, width), F32),
        pltpu.VMEM((2, width, width), BF16),
        pltpu.VMEM((2, width, width), BF16),
        pltpu.VMEM((16, width), jnp.int32),
        pltpu.VMEM((16, width), jnp.int32),
        pltpu.VMEM((2, half, columns), BF16),
        pltpu.VMEM((2, half, columns), BF16),
        pltpu.VMEM((others, 2, half, width), BF16),
        pltpu.VMEM((others, 2, half, width), BF16),
        pltpu.VMEM((n_depth, 2, 2, half, width), BF16),
        pltpu.VMEM((2, width, width), F32),
        pltpu.VMEM((n_depth + 1, 2, width, width), BF16),
        pltpu.VMEM((2, width, width), F32),
        pltpu.VMEM((2, width, width), BF16),
        pltpu.VMEM((2, width, width), BF16),
        pltpu.VMEM((n_depth, 2, 2, half, width), BF16),
        pltpu.VMEM((n_depth, 2, 2, half, width), BF16),
        pltpu.VMEM((2, half, columns), BF16),
        pltpu.VMEM((2, half, columns), BF16),
        pltpu.VMEM((2, half, columns), BF16),
        pltpu.VMEM((2, half, columns), BF16),
        dma((10,)),
        dma((2,)),
        dma((2, 4)),
        dma((2, 4)),
        dma((2,)),
        dma((others,)),
        dma((others,)),
        dma((others, 4)),
        dma((others, 4)),
        dma((others,)),
        dma((others,)),
        dma((others, 4)),
        dma((others, 4)),
        dma((2, 4)),
        dma((2, 4)),
    ]
    anywhere = pl.BlockSpec(memory_space=pltpu.HBM)
    return pl.pallas_call(
        kernel,
        out_shape=pltpu.VMEM(transmission.shape, F32),
        in_specs=[anywhere] * 9,
        out_specs=pl.BlockSpec(memory_space=pltpu.VMEM),
        scratch_shapes=scratch,
        compiler_params=pltpu.CompilerParams(
            collective_id=0, has_side_effects=True, vmem_limit_bytes=57_000_000
        ),
    )(transmission, probe_wave, prop_phase, measured, scan_rows, scan_cols, live_counts, t1, t2)


def solution(mesh):
    in_specs = (
        P("depth", None, "scan", None),
        P(),
        P(),
        P("scan", None, None),
        P("scan"),
        P("scan"),
        P("scan"),
    )
    out_specs = P("depth", None, "scan", None)
    return jax.shard_map(body, mesh=mesh, in_specs=in_specs, out_specs=out_specs, check_vma=False)
```

```python
import functools
import math

import jax
import jax.numpy as jnp
import numpy as np
from jax import lax
from jax.experimental import pallas as pl
from jax.experimental.pallas import tpu as pltpu
from jax.sharding import PartitionSpec as P

MESH = pl.DeviceIdType.MESH
BF16 = jnp.bfloat16
F32 = jnp.float32


def dft_blocks(pixels):
    index = np.arange(pixels)
    angles = (index[:, None] * index[None, :] % pixels) * (2.0 * math.pi / pixels)
    scale = 1.0 / math.sqrt(pixels)
    re, im = np.cos(angles) * scale, -np.sin(angles) * scale
    blocks = []
    for parity in range(2):
        r, i = re[parity::2, : pixels // 2], im[parity::2, : pixels // 2]
        blocks.append(np.block([[r, -i], [i, r]]))
    blocks = np.stack(blocks)
    return jnp.asarray(blocks, F32).astype(BF16), jnp.asarray(blocks.swapaxes(1, 2), F32).astype(BF16)


def kernel(
    tile_hbm, probe_hbm, phase_hbm, meas_hbm, rows_hbm, cols_hbm, live_hbm, t1_hbm, t2_hbm,
    out_ref,
    rows_s, cols_s, live_s, blk, low, tile32, tile16, probe32, phase, meas_in, meas_out, meas, t1, t2, par_out, par_in,
    lower, upper, crops_b, crops_a, patch, prop, psi, adjoint, xs, us, grads, came,
    strip_low, strip_high, got_low, got_high,
    load_sem, par_sem, tile_sem_s, tile_sem_r, meas_sem,
    bx_s, bx_r, ax_s, ax_r, gb_s, gb_r, ga_s, ga_r, strip_s, strip_r,
):
    depth = lax.axis_index("depth")
    scan = lax.axis_index("scan")
    n_depth = lax.axis_size("depth")
    n_scan = lax.axis_size("scan")
    after = lax.rem(scan + 1, n_scan)
    before = lax.rem(scan + n_scan - 1, n_scan)
    half, width = patch.shape[3], patch.shape[4]
    blocks = tile32.shape[2] // width
    slots = n_depth
    rows = half // 2
    order = (n_depth // 2, *(at for at in range(1, n_depth) if at != n_depth // 2), 0)
    chunks = [(plane, slice(part * rows, (part + 1) * rows)) for plane in range(2) for part in range(2)]

    def peer(offset):
        return (lax.rem(depth + offset, n_depth), scan)

    barrier = pltpu.get_barrier_semaphore()
    for offset in range(1, n_depth):
        pl.semaphore_signal(barrier, inc=1, device_id=peer(offset), device_id_type=MESH)
    pl.semaphore_signal(barrier, inc=1, device_id=(depth, after), device_id_type=MESH)
    pl.semaphore_signal(barrier, inc=1, device_id=(depth, before), device_id_type=MESH)
    loads = [
        pltpu.make_async_copy(tile_hbm.at[0, 0], tile32.at[0], load_sem.at[0]),
        pltpu.make_async_copy(tile_hbm.at[0, 1], tile32.at[1], load_sem.at[1]),
        pltpu.make_async_copy(probe_hbm, probe32, load_sem.at[2]),
        pltpu.make_async_copy(phase_hbm, phase, load_sem.at[3]),
        pltpu.make_async_copy(t1_hbm, t1, load_sem.at[4]),
        pltpu.make_async_copy(t2_hbm, t2, load_sem.at[5]),
        pltpu.make_async_copy(rows_hbm, rows_s, load_sem.at[6]),
        pltpu.make_async_copy(cols_hbm, cols_s, load_sem.at[7]),
        pltpu.make_async_copy(live_hbm, live_s, load_sem.at[8]),
        pltpu.make_async_copy(meas_hbm.at[depth], meas_in, load_sem.at[9]),
    ]
    for at in (6, 7, 8, 0, 1, 9, 3, 2, 4, 5):
        loads[at].start()

    for load in loads[6:9]:
        load.wait()
    for slot in range(slots):
        par_out[slot : slot + 1, :] = jnp.full((1, width), rows_s[slot], jnp.int32)
        par_out[slots + slot : slots + slot + 1, :] = jnp.full((1, width), cols_s[slot], jnp.int32)
    par_out[2 * slots : 2 * slots + 1, :] = jnp.full((1, width), live_s[0], jnp.int32)
    pl.semaphore_wait(barrier, n_depth + 1)

    def send(src, dst, s_sem, r_sem, device):
        return pltpu.make_async_remote_copy(
            src_ref=src, dst_ref=dst, send_sem=s_sem, recv_sem=r_sem,
            device_id=device, device_id_type=MESH,
        )

    par_copy = send(par_out, par_in, par_sem.at[0], par_sem.at[1], (depth, after))
    par_copy.start()
    tile_copies = []
    for at, (plane, span) in enumerate(chunks):
        if at % 2 == 0:
            loads[plane].wait()
        tile16[plane, span] = tile32[plane, span].astype(BF16)
        pair = [
            send(tile16.at[plane, span], lower.at[plane, span], tile_sem_s.at[0, at],
                 tile_sem_r.at[0, at], (depth, after)),
            send(tile16.at[plane, span], upper.at[plane, span], tile_sem_s.at[1, at],
                 tile_sem_r.at[1, at], (depth, before)),
        ]
        for copy in pair:
            copy.start()
        tile_copies.append(pair)
    par_copy.wait_recv()
    row_at = lax.broadcasted_iota(jnp.int32, (half, width), 0)
    lane_at = lax.broadcasted_iota(jnp.int32, (rows, width), 1)
    for slot in range(slots):
        first = jnp.broadcast_to(par_in[slots + slot : slots + slot + 1, :], (rows, width))
        block = (first >> 8) + jnp.where(lane_at < (first & (width - 1)), 1, 0)
        blk[slot] = block.astype(F32).astype(BF16)

    def pick(slot, values):
        piece = values[0]
        for at in range(1, blocks):
            piece = jnp.where(blk[slot] == at, values[at], piece)
        return piece

    def columns(at):
        return slice(at * width, (at + 1) * width)

    b_copies = []
    for offset in order:
        slot = lax.rem(depth + offset, n_depth)
        for plane, span in chunks:
            piece = pick(slot, [tile16[plane, span, columns(at)] for at in range(blocks)])
            if offset == 0:
                patch[depth, 1, plane, span] = piece
            else:
                crops_b[offset - 1, plane, span] = piece
        if offset:
            copy = send(crops_b.at[offset - 1], patch.at[depth, 1], bx_s.at[offset - 1],
                        bx_r.at[offset - 1], peer(offset))
            copy.start()
            b_copies.append(copy)

    for slot in range(slots):
        begin = jnp.broadcast_to(par_in[slot : slot + 1, :], (half, width))
        low[slot] = jnp.where(row_at >= begin, 1.0, 0.0).astype(BF16)

    big_row = lax.broadcasted_iota(jnp.int32, (width, width), 0)
    big_lane = lax.broadcasted_iota(jnp.int32, (width, width), 1)
    to_split = jnp.where(2 * (big_row & (half - 1)) + (big_row // half) == big_lane, 1.0, 0.0).astype(BF16)
    of_split = jnp.where(2 * (big_lane & (half - 1)) + (big_lane // half) == big_row, 1.0, 0.0).astype(BF16)

    def split_order(value, parts):
        total = jnp.zeros_like(value)
        for _ in range(parts):
            part = value.astype(BF16)
            value = value - part.astype(F32)
            moved = jnp.dot(to_split, part, preferred_element_type=F32).astype(BF16)
            total = total + jnp.dot(moved, of_split, preferred_element_type=F32)
        return total

    loads[9].wait()
    meas_out[...] = split_order(meas_in[...], 3)
    meas_copy = send(meas_out, meas, meas_sem.at[0], meas_sem.at[1], (depth, after))
    meas_copy.start()
    loads[3].wait()
    phase[...] = split_order(phase[...], 3)
    prop[0] = jnp.cos(phase[...])

    loads[2].wait()
    own_row = jnp.broadcast_to(par_in[pl.ds(depth, 1), :], (width, width))
    own_col = jnp.broadcast_to(par_in[pl.ds(slots + depth, 1), :], (width, width))
    down = jnp.where(((big_row - own_row) & (width - 1)) == big_lane, 1.0, 0.0).astype(BF16)
    across = jnp.where(((big_row + own_col) & (width - 1)) == big_lane, 1.0, 0.0).astype(BF16)
    for plane in range(2):
        rolled = jnp.dot(down, probe32[plane].astype(BF16), preferred_element_type=F32)
        rolled = jnp.dot(rolled.astype(BF16), across, preferred_element_type=F32)
        psi[0, plane] = rolled.astype(BF16)

    a_copies = []
    for number, (plane, span) in enumerate(chunks):
        for copy in tile_copies[number]:
            copy.wait_recv()
        for offset in order:
            slot = lax.rem(depth + offset, n_depth)
            is_low = low[slot, span] > 0.5
            piece = pick(slot, [
                jnp.where(is_low, lower[plane, span, columns(at)], upper[plane, span, columns(at)])
                for at in range(blocks)
            ])
            if offset == 0:
                patch[depth, 0, plane, span] = piece
            else:
                crops_a[offset - 1, plane, span] = piece
                copy = send(crops_a.at[offset - 1, plane, span], patch.at[depth, 0, plane, span],
                            ax_s.at[offset - 1, number], ax_r.at[offset - 1, number],
                            peer(offset))
                copy.start()
                a_copies.append(copy)

    prop[1] = jnp.sin(phase[...])
    loads[4].wait()
    loads[5].wait()
    sides = [slice(0, half), slice(half, width)]

    def to_frequencies(upper_re, upper_im, lower_re, lower_im):
        xs[0, :half] = (upper_re + lower_re).astype(BF16)
        xs[0, half:] = (upper_im + lower_im).astype(BF16)
        xs[1, :half] = (upper_re - lower_re).astype(BF16)
        xs[1, half:] = (upper_im - lower_im).astype(BF16)
        for parity in range(2):
            inner = jnp.dot(t1[parity], xs[parity], preferred_element_type=F32)
            for part in range(2):
                left, right = inner[sides[part], :half], inner[sides[part], half:]
                us[0, sides[parity], sides[part]] = (left + right).astype(BF16)
                us[1, sides[parity], sides[part]] = (left - right).astype(BF16)
        return [
            jnp.dot(us[parity], t2[parity], preferred_element_type=F32) for parity in range(2)
        ]

    def keep(parity, re, im):
        for part in range(2):
            xs[part, :half, sides[parity]] = re[sides[part]].astype(BF16)
            xs[part, half:, sides[parity]] = im[sides[part]].astype(BF16)

    def to_positions():
        even = jnp.dot(t2[0], xs[0], preferred_element_type=F32)
        odd = jnp.dot(t2[1], xs[1], preferred_element_type=F32)
        for part in range(2):
            upper_half = (even[sides[part]] + odd[sides[part]]).astype(BF16)
            lower_half = (even[sides[part]] - odd[sides[part]]).astype(BF16)
            for parity in range(2):
                us[parity, :half, sides[part]] = upper_half[:, sides[parity]]
                us[parity, half:, sides[part]] = lower_half[:, sides[parity]]
        even = jnp.dot(us[0], t1[0], preferred_element_type=F32)
        odd = jnp.dot(us[1], t1[1], preferred_element_type=F32)
        return [
            jnp.concatenate([even[:, side] + odd[:, side], even[:, side] - odd[:, side]], axis=1)
            for side in sides
        ]

    def propagate(halves, sign):
        both = to_frequencies(*halves)
        for parity in range(2):
            re, im = both[parity][:, :half], both[parity][:, half:]
            pr, pi = prop[0, :, sides[parity]], sign * prop[1, :, sides[parity]]
            keep(parity, re * pr - im * pi, re * pi + im * pr)
        return to_positions()

    def forward(at, carry):
        @pl.when(at != depth)
        def _():
            offset = lax.rem(depth + n_depth - at, n_depth) - 1
            send(crops_b.at[offset], patch.at[at, 1], bx_s.at[offset], bx_r.at[offset],
                 (at, scan)).wait_recv()
            for number, (plane, rows_at) in enumerate(chunks):
                send(crops_a.at[offset, plane, rows_at], patch.at[at, 0, plane, rows_at],
                     ax_s.at[offset, number], ax_r.at[offset, number],
                     (at, scan)).wait_recv()

        halves = []
        for part in range(2):
            tr, ti = patch[at, part, 0].astype(F32), patch[at, part, 1].astype(F32)
            pr, pi = psi[at, 0, sides[part]].astype(F32), psi[at, 1, sides[part]].astype(F32)
            halves += [tr * pr - ti * pi, tr * pi + ti * pr]
        re, im = propagate(halves, 1.0)
        psi[at + 1, 0] = re.astype(BF16)
        psi[at + 1, 1] = im.astype(BF16)
        return carry

    lax.fori_loop(0, n_depth, forward, 0)

    leaving = [psi[n_depth, plane, side].astype(F32) for side in sides for plane in range(2)]
    both = to_frequencies(*leaving)
    meas_copy.wait_recv()
    live = jnp.where(
        jnp.broadcast_to(par_in[2 * slots : 2 * slots + 1, :half], (width, half)) > depth, 1.0, 0.0
    )
    for parity in range(2):
        re, im = both[parity][:, :half], both[parity][:, half:]
        factor = live * (1.0 - meas[:, sides[parity]] * lax.rsqrt(re * re + im * im + 1.0))
        keep(parity, factor * re, factor * im)
    re, im = to_positions()
    adjoint[0] = re
    adjoint[1] = im

    def grad_near(at):
        offset = lax.rem(at + n_depth - depth, n_depth) - 1
        return [
            send(grads.at[at, 0, plane, span], came.at[depth, 0, plane, span],
                 ga_s.at[offset, number], ga_r.at[offset, number], (at, scan))
            for number, (plane, span) in enumerate(chunks)
        ]

    def grad_far(at):
        offset = lax.rem(at + n_depth - depth, n_depth) - 1
        return send(grads.at[at, 1], came.at[depth, 1], gb_s.at[offset], gb_r.at[offset],
                    (at, scan))

    def backward(step, carry):
        at = n_depth - 1 - step
        mu_re, mu_im = propagate([adjoint[plane, side] for side in sides for plane in range(2)], -1.0)
        for part in range(2):
            re, im = mu_re[sides[part]], mu_im[sides[part]]
            tr, ti = patch[at, part, 0].astype(F32), patch[at, part, 1].astype(F32)
            pr, pi = psi[at, 0, sides[part]].astype(F32), psi[at, 1, sides[part]].astype(F32)
            grads[at, part, 0] = (pr * re + pi * im).astype(BF16)
            grads[at, part, 1] = (pr * im - pi * re).astype(BF16)
            adjoint[0, sides[part]] = tr * re + ti * im
            adjoint[1, sides[part]] = tr * im - ti * re
            if part == 0:

                @pl.when(at != depth)
                def _():
                    for copy in grad_near(at):
                        copy.start()

        return carry

    lax.fori_loop(0, n_depth, backward, 0)

    for back in range(n_depth):
        at = n_depth - 1 - back

        @pl.when(at != depth)
        def _(at=at):
            grad_far(at).start()

    for part in range(2):
        for plane in range(2):
            came[depth, part, plane] = grads[depth, part, plane]
    zero = jnp.zeros((rows // 2, width), BF16)
    strip_copies = []
    for number, (plane, span) in enumerate(chunks):
        for offset in range(n_depth - 1):
            send(grads.at[0, 0, plane, span], came.at[0, 0, plane, span], ga_s.at[offset, number],
                 ga_r.at[offset, number], (depth, scan)).wait_recv()
        for piece in range(2):
            start = span.start + piece * (rows // 2)
            at_rows = slice(start, start + rows // 2)
            lows, highs = [], []
            for slot in range(slots):
                value = came[slot, 0, plane, at_rows]
                is_low = low[slot, at_rows] > 0.5
                lows.append(jnp.where(is_low, value, zero))
                highs.append(jnp.where(is_low, zero, value))
            for at in range(blocks):
                for target, values in ((strip_low, lows), (strip_high, highs)):
                    terms = [
                        jnp.where(blk[slot, : rows // 2] == at, values[slot], zero)
                        for slot in range(slots)
                    ]
                    total = (terms[0] + terms[1]) + (terms[2] + terms[3])
                    target[plane, at_rows, columns(at)] = total
        pair = [
            send(strip_low.at[plane, span], got_low.at[plane, span], strip_s.at[0, number],
                 strip_r.at[0, number], (depth, before)),
            send(strip_high.at[plane, span], got_high.at[plane, span], strip_s.at[1, number],
                 strip_r.at[1, number], (depth, after)),
        ]
        for copy in pair:
            copy.start()
        strip_copies.append(pair)

    for offset in range(n_depth - 1):
        send(grads.at[0, 1], came.at[0, 1], gb_s.at[offset], gb_r.at[offset],
             (depth, scan)).wait_recv()
    for plane in range(2):
        for piece in range(4):
            at_rows = slice(piece * (rows // 2), (piece + 1) * (rows // 2))
            values = [came[slot, 1, plane, at_rows] for slot in range(slots)]
            for at in range(blocks):
                terms = [
                    jnp.where(blk[slot, : rows // 2] == at, values[slot], zero).astype(F32)
                    for slot in range(slots)
                ]
                total = (terms[0] + terms[1]) + (terms[2] + terms[3])
                out_ref[0, plane, at_rows, columns(at)] = total
    for number, (plane, span) in enumerate(chunks):
        for copy in strip_copies[number]:
            copy.wait_recv()
        out_ref[0, plane, span] = out_ref[0, plane, span] + (
            got_low[plane, span].astype(F32) + got_high[plane, span].astype(F32)
        )

    par_copy.wait_send()
    meas_copy.wait_send()
    for copy in b_copies + a_copies:
        copy.wait_send()
    for pair in tile_copies + strip_copies:
        for copy in pair:
            copy.wait_send()
    for step in range(1, n_depth):
        at = lax.rem(depth + step, n_depth)
        for copy in grad_near(at) + [grad_far(at)]:
            copy.wait_send()


def body(transmission, probe_wave, prop_phase, measured, scan_rows, scan_cols, live_counts):
    width = probe_wave.shape[-1]
    half = transmission.shape[2]
    columns = transmission.shape[3]
    n_depth = lax.axis_size("depth")
    t1, t2 = dft_blocks(width)
    dma = pltpu.SemaphoreType.DMA
    others = n_depth - 1
    scratch = [
        pltpu.SMEM((n_depth,), jnp.int32),
        pltpu.SMEM((n_depth,), jnp.int32),
        pltpu.SMEM((1,), jnp.int32),
        pltpu.VMEM((n_depth, half // 2, width), BF16),
        pltpu.VMEM((n_depth, half, width), BF16),
        pltpu.VMEM((2, half, columns), F32),
        pltpu.VMEM((2, half, columns), BF16),
        pltpu.VMEM((2, width, width), F32),
        pltpu.VMEM((width, width), F32),
        pltpu.VMEM((width, width), F32),
        pltpu.VMEM((width, width), F32),
        pltpu.VMEM((width, width), F32),
        pltpu.VMEM((2, width, width), BF16),
        pltpu.VMEM((2, width, width), BF16),
        pltpu.VMEM((16, width), jnp.int32),
        pltpu.VMEM((16, width), jnp.int32),
        pltpu.VMEM((2, half, columns), BF16),
        pltpu.VMEM((2, half, columns), BF16),
        pltpu.VMEM((others, 2, half, width), BF16),
        pltpu.VMEM((others, 2, half, width), BF16),
        pltpu.VMEM((n_depth, 2, 2, half, width), BF16),
        pltpu.VMEM((2, width, width), F32),
        pltpu.VMEM((n_depth + 1, 2, width, width), BF16),
        pltpu.VMEM((2, width, width), F32),
        pltpu.VMEM((2, width, width), BF16),
        pltpu.VMEM((2, width, width), BF16),
        pltpu.VMEM((n_depth, 2, 2, half, width), BF16),
        pltpu.VMEM((n_depth, 2, 2, half, width), BF16),
        pltpu.VMEM((2, half, columns), BF16),
        pltpu.VMEM((2, half, columns), BF16),
        pltpu.VMEM((2, half, columns), BF16),
        pltpu.VMEM((2, half, columns), BF16),
        dma((10,)),
        dma((2,)),
        dma((2, 4)),
        dma((2, 4)),
        dma((2,)),
        dma((others,)),
        dma((others,)),
        dma((others, 4)),
        dma((others, 4)),
        dma((others,)),
        dma((others,)),
        dma((others, 4)),
        dma((others, 4)),
        dma((2, 4)),
        dma((2, 4)),
    ]
    anywhere = pl.BlockSpec(memory_space=pltpu.HBM)
    return pl.pallas_call(
        kernel,
        out_shape=pltpu.VMEM(transmission.shape, F32),
        in_specs=[anywhere] * 9,
        out_specs=pl.BlockSpec(memory_space=pltpu.VMEM),
        scratch_shapes=scratch,
        compiler_params=pltpu.CompilerParams(
            collective_id=0, has_side_effects=True, vmem_limit_bytes=57_000_000
        ),
    )(transmission, probe_wave, prop_phase, measured, scan_rows, scan_cols, live_counts, t1, t2)


def solution(mesh):
    in_specs = (
        P("depth", None, "scan", None),
        P(),
        P(),
        P("scan", None, None),
        P("scan"),
        P("scan"),
        P("scan"),
    )
    out_specs = P("depth", None, "scan", None)
    return jax.shard_map(body, mesh=mesh, in_specs=in_specs, out_specs=out_specs, check_vma=False)
```

```python
import functools
import math

import jax
import jax.numpy as jnp
import numpy as np
from jax import lax
from jax.experimental import pallas as pl
from jax.experimental.pallas import tpu as pltpu
from jax.sharding import PartitionSpec as P

MESH = pl.DeviceIdType.MESH
BF16 = jnp.bfloat16
F32 = jnp.float32


def dft_blocks(pixels):
    index = np.arange(pixels)
    angles = (index[:, None] * index[None, :] % pixels) * (2.0 * math.pi / pixels)
    scale = 1.0 / math.sqrt(pixels)
    re, im = np.cos(angles) * scale, -np.sin(angles) * scale
    blocks = []
    for parity in range(2):
        r, i = re[parity::2, : pixels // 2], im[parity::2, : pixels // 2]
        blocks.append(np.block([[r, -i], [i, r]]))
    blocks = np.stack(blocks)
    return jnp.asarray(blocks, F32).astype(BF16), jnp.asarray(blocks.swapaxes(1, 2), F32).astype(BF16)


def kernel(
    tile_hbm, probe_hbm, phase_hbm, meas_hbm, rows_hbm, cols_hbm, live_hbm, t1_hbm, t2_hbm,
    out_ref,
    rows_s, cols_s, live_s, blk, low, tile32, tile16, probe32, phase, meas_in, meas_out, meas, t1, t2, par_out, par_in,
    lower, upper, crops_b, crops_a, patch, prop, psi, adjoint, xs, us, grads, came,
    strip_low, strip_high, got_low, got_high,
    load_sem, par_sem, tile_sem_s, tile_sem_r, meas_sem,
    bx_s, bx_r, ax_s, ax_r, gb_s, gb_r, ga_s, ga_r, strip_s, strip_r,
):
    depth = lax.axis_index("depth")
    scan = lax.axis_index("scan")
    n_depth = lax.axis_size("depth")
    n_scan = lax.axis_size("scan")
    after = lax.rem(scan + 1, n_scan)
    before = lax.rem(scan + n_scan - 1, n_scan)
    half, width = patch.shape[3], patch.shape[4]
    blocks = tile32.shape[2] // width
    slots = n_depth
    rows = half // 2
    order = (n_depth // 2, *(at for at in range(1, n_depth) if at != n_depth // 2), 0)
    chunks = [(plane, slice(part * rows, (part + 1) * rows)) for plane in range(2) for part in range(2)]

    def peer(offset):
        return (lax.rem(depth + offset, n_depth), scan)

    barrier = pltpu.get_barrier_semaphore()
    for offset in range(1, n_depth):
        pl.semaphore_signal(barrier, inc=1, device_id=peer(offset), device_id_type=MESH)
    pl.semaphore_signal(barrier, inc=1, device_id=(depth, after), device_id_type=MESH)
    pl.semaphore_signal(barrier, inc=1, device_id=(depth, before), device_id_type=MESH)
    loads = [
        pltpu.make_async_copy(tile_hbm.at[0, 0], tile32.at[0], load_sem.at[0]),
        pltpu.make_async_copy(tile_hbm.at[0, 1], tile32.at[1], load_sem.at[1]),
        pltpu.make_async_copy(probe_hbm, probe32, load_sem.at[2]),
        pltpu.make_async_copy(phase_hbm, phase, load_sem.at[3]),
        pltpu.make_async_copy(t1_hbm, t1, load_sem.at[4]),
        pltpu.make_async_copy(t2_hbm, t2, load_sem.at[5]),
        pltpu.make_async_copy(rows_hbm, rows_s, load_sem.at[6]),
        pltpu.make_async_copy(cols_hbm, cols_s, load_sem.at[7]),
        pltpu.make_async_copy(live_hbm, live_s, load_sem.at[8]),
        pltpu.make_async_copy(meas_hbm.at[depth], meas_in, load_sem.at[9]),
    ]
    for at in (6, 7, 8, 0, 1, 9, 3, 2, 4, 5):
        loads[at].start()

    for load in loads[6:9]:
        load.wait()
    for slot in range(slots):
        par_out[slot : slot + 1, :] = jnp.full((1, width), rows_s[slot], jnp.int32)
        par_out[slots + slot : slots + slot + 1, :] = jnp.full((1, width), cols_s[slot], jnp.int32)
    par_out[2 * slots : 2 * slots + 1, :] = jnp.full((1, width), live_s[0], jnp.int32)
    pl.semaphore_wait(barrier, n_depth + 1)

    def send(src, dst, s_sem, r_sem, device):
        return pltpu.make_async_remote_copy(
            src_ref=src, dst_ref=dst, send_sem=s_sem, recv_sem=r_sem,
            device_id=device, device_id_type=MESH,
        )

    par_copy = send(par_out, par_in, par_sem.at[0], par_sem.at[1], (depth, after))
    par_copy.start()
    tile_copies = []
    for at, (plane, span) in enumerate(chunks):
        if at % 2 == 0:
            loads[plane].wait()
        tile16[plane, span] = tile32[plane, span].astype(BF16)
        pair = [
            send(tile16.at[plane, span], lower.at[plane, span], tile_sem_s.at[0, at],
                 tile_sem_r.at[0, at], (depth, after)),
            send(tile16.at[plane, span], upper.at[plane, span], tile_sem_s.at[1, at],
                 tile_sem_r.at[1, at], (depth, before)),
        ]
        for copy in pair:
            copy.start()
        tile_copies.append(pair)
    par_copy.wait_recv()
    row_at = lax.broadcasted_iota(jnp.int32, (half, width), 0)
    lane_at = lax.broadcasted_iota(jnp.int32, (rows, width), 1)
    for slot in range(slots):
        first = jnp.broadcast_to(par_in[slots + slot : slots + slot + 1, :], (rows, width))
        block = (first >> 8) + jnp.where(lane_at < (first & (width - 1)), 1, 0)
        blk[slot] = block.astype(F32).astype(BF16)

    def pick(slot, values):
        piece = values[0]
        for at in range(1, blocks):
            piece = jnp.where(blk[slot] == at, values[at], piece)
        return piece

    def columns(at):
        return slice(at * width, (at + 1) * width)

    b_copies = []
    for offset in order:
        slot = lax.rem(depth + offset, n_depth)
        for plane, span in chunks:
            piece = pick(slot, [tile16[plane, span, columns(at)] for at in range(blocks)])
            if offset == 0:
                patch[depth, 1, plane, span] = piece
            else:
                crops_b[offset - 1, plane, span] = piece
        if offset:
            copy = send(crops_b.at[offset - 1], patch.at[depth, 1], bx_s.at[offset - 1],
                        bx_r.at[offset - 1], peer(offset))
            copy.start()
            b_copies.append(copy)

    for slot in range(slots):
        begin = jnp.broadcast_to(par_in[slot : slot + 1, :], (half, width))
        low[slot] = jnp.where(row_at >= begin, 1.0, 0.0).astype(BF16)

    big_row = lax.broadcasted_iota(jnp.int32, (width, width), 0)
    big_lane = lax.broadcasted_iota(jnp.int32, (width, width), 1)
    to_split = jnp.where(2 * (big_row & (half - 1)) + (big_row // half) == big_lane, 1.0, 0.0).astype(BF16)
    of_split = jnp.where(2 * (big_lane & (half - 1)) + (big_lane // half) == big_row, 1.0, 0.0).astype(BF16)

    def split_order(value, parts):
        total = jnp.zeros_like(value)
        for _ in range(parts):
            part = value.astype(BF16)
            value = value - part.astype(F32)
            moved = jnp.dot(to_split, part, preferred_element_type=F32).astype(BF16)
            total = total + jnp.dot(moved, of_split, preferred_element_type=F32)
        return total

    loads[9].wait()
    meas_out[...] = split_order(meas_in[...], 3)
    meas_copy = send(meas_out, meas, meas_sem.at[0], meas_sem.at[1], (depth, after))
    meas_copy.start()
    loads[3].wait()
    phase[...] = split_order(phase[...], 3)
    prop[0] = jnp.cos(phase[...])

    loads[2].wait()
    own_row = jnp.broadcast_to(par_in[pl.ds(depth, 1), :], (width, width))
    own_col = jnp.broadcast_to(par_in[pl.ds(slots + depth, 1), :], (width, width))
    down = jnp.where(((big_row - own_row) & (width - 1)) == big_lane, 1.0, 0.0).astype(BF16)
    across = jnp.where(((big_row + own_col) & (width - 1)) == big_lane, 1.0, 0.0).astype(BF16)
    for plane in range(2):
        rolled = jnp.dot(down, probe32[plane].astype(BF16), preferred_element_type=F32)
        rolled = jnp.dot(rolled.astype(BF16), across, preferred_element_type=F32)
        psi[0, plane] = rolled.astype(BF16)

    a_copies = []
    for number, (plane, span) in enumerate(chunks):
        for copy in tile_copies[number]:
            copy.wait_recv()
        for offset in order:
            slot = lax.rem(depth + offset, n_depth)
            is_low = low[slot, span] > 0.5
            piece = pick(slot, [
                jnp.where(is_low, lower[plane, span, columns(at)], upper[plane, span, columns(at)])
                for at in range(blocks)
            ])
            if offset == 0:
                patch[depth, 0, plane, span] = piece
            else:
                crops_a[offset - 1, plane, span] = piece
                copy = send(crops_a.at[offset - 1, plane, span], patch.at[depth, 0, plane, span],
                            ax_s.at[offset - 1, number], ax_r.at[offset - 1, number],
                            peer(offset))
                copy.start()
                a_copies.append(copy)

    prop[1] = jnp.sin(phase[...])
    loads[4].wait()
    loads[5].wait()
    sides = [slice(0, half), slice(half, width)]

    def to_frequencies(upper_re, upper_im, lower_re, lower_im):
        xs[0, :half] = (upper_re + lower_re).astype(BF16)
        xs[0, half:] = (upper_im + lower_im).astype(BF16)
        xs[1, :half] = (upper_re - lower_re).astype(BF16)
        xs[1, half:] = (upper_im - lower_im).astype(BF16)
        for parity in range(2):
            inner = jnp.dot(t1[parity], xs[parity], preferred_element_type=F32)
            for part in range(2):
                left, right = inner[sides[part], :half], inner[sides[part], half:]
                us[0, sides[parity], sides[part]] = (left + right).astype(BF16)
                us[1, sides[parity], sides[part]] = (left - right).astype(BF16)
        return [
            jnp.dot(us[parity], t2[parity], preferred_element_type=F32) for parity in range(2)
        ]

    def keep(parity, re, im):
        for part in range(2):
            xs[part, :half, sides[parity]] = re[sides[part]].astype(BF16)
            xs[part, half:, sides[parity]] = im[sides[part]].astype(BF16)

    def to_positions():
        even = jnp.dot(t2[0], xs[0], preferred_element_type=F32)
        odd = jnp.dot(t2[1], xs[1], preferred_element_type=F32)
        for part in range(2):
            upper_half = (even[sides[part]] + odd[sides[part]]).astype(BF16)
            lower_half = (even[sides[part]] - odd[sides[part]]).astype(BF16)
            for parity in range(2):
                us[parity, :half, sides[part]] = upper_half[:, sides[parity]]
                us[parity, half:, sides[part]] = lower_half[:, sides[parity]]
        even = jnp.dot(us[0], t1[0], preferred_element_type=F32)
        odd = jnp.dot(us[1], t1[1], preferred_element_type=F32)
        return [
            jnp.concatenate([even[:, side] + odd[:, side], even[:, side] - odd[:, side]], axis=1)
            for side in sides
        ]

    def propagate(halves, sign):
        both = to_frequencies(*halves)
        for parity in range(2):
            re, im = both[parity][:, :half], both[parity][:, half:]
            pr, pi = prop[0, :, sides[parity]], sign * prop[1, :, sides[parity]]
            keep(parity, re * pr - im * pi, re * pi + im * pr)
        return to_positions()

    def forward(at, carry):
        @pl.when(at != depth)
        def _():
            offset = lax.rem(depth + n_depth - at, n_depth) - 1
            send(crops_b.at[offset], patch.at[at, 1], bx_s.at[offset], bx_r.at[offset],
                 (at, scan)).wait_recv()
            for number, (plane, rows_at) in enumerate(chunks):
                send(crops_a.at[offset, plane, rows_at], patch.at[at, 0, plane, rows_at],
                     ax_s.at[offset, number], ax_r.at[offset, number],
                     (at, scan)).wait_recv()

        halves = []
        for part in range(2):
            tr, ti = patch[at, part, 0].astype(F32), patch[at, part, 1].astype(F32)
            pr, pi = psi[at, 0, sides[part]].astype(F32), psi[at, 1, sides[part]].astype(F32)
            halves += [tr * pr - ti * pi, tr * pi + ti * pr]
        re, im = propagate(halves, 1.0)
        psi[at + 1, 0] = re.astype(BF16)
        psi[at + 1, 1] = im.astype(BF16)
        return carry

    lax.fori_loop(0, n_depth, forward, 0)

    leaving = [psi[n_depth, plane, side].astype(F32) for side in sides for plane in range(2)]
    both = to_frequencies(*leaving)
    meas_copy.wait_recv()
    live = jnp.where(
        jnp.broadcast_to(par_in[2 * slots : 2 * slots + 1, :half], (width, half)) > depth, 1.0, 0.0
    )
    for parity in range(2):
        re, im = both[parity][:, :half], both[parity][:, half:]
        factor = live * (1.0 - meas[:, sides[parity]] * lax.rsqrt(re * re + im * im + 1.0))
        keep(parity, factor * re, factor * im)
    re, im = to_positions()
    adjoint[0] = re
    adjoint[1] = im

    def grad_near(at):
        offset = lax.rem(at + n_depth - depth, n_depth) - 1
        return [
            send(grads.at[at, 0, plane, span], came.at[depth, 0, plane, span],
                 ga_s.at[offset, number], ga_r.at[offset, number], (at, scan))
            for number, (plane, span) in enumerate(chunks)
        ]

    def grad_far(at):
        offset = lax.rem(at + n_depth - depth, n_depth) - 1
        return send(grads.at[at, 1], came.at[depth, 1], gb_s.at[offset], gb_r.at[offset],
                    (at, scan))

    def backward(step, carry):
        at = n_depth - 1 - step
        mu_re, mu_im = propagate([adjoint[plane, side] for side in sides for plane in range(2)], -1.0)
        for part in range(2):
            re, im = mu_re[sides[part]], mu_im[sides[part]]
            tr, ti = patch[at, part, 0].astype(F32), patch[at, part, 1].astype(F32)
            pr, pi = psi[at, 0, sides[part]].astype(F32), psi[at, 1, sides[part]].astype(F32)
            grads[at, part, 0] = (pr * re + pi * im).astype(BF16)
            grads[at, part, 1] = (pr * im - pi * re).astype(BF16)
            adjoint[0, sides[part]] = tr * re + ti * im
            adjoint[1, sides[part]] = tr * im - ti * re
            if part == 0:

                @pl.when(at != depth)
                def _():
                    for copy in grad_near(at):
                        copy.start()

        return carry

    lax.fori_loop(0, n_depth, backward, 0)

    for back in range(n_depth):
        at = n_depth - 1 - back

        @pl.when(at != depth)
        def _(at=at):
            grad_far(at).start()

    for part in range(2):
        for plane in range(2):
            came[depth, part, plane] = grads[depth, part, plane]
    zero = jnp.zeros((rows // 2, width), BF16)
    strip_copies = []
    for number, (plane, span) in enumerate(chunks):
        for offset in range(n_depth - 1):
            send(grads.at[0, 0, plane, span], came.at[0, 0, plane, span], ga_s.at[offset, number],
                 ga_r.at[offset, number], (depth, scan)).wait_recv()
        pair = [
            send(strip_low.at[plane, span], got_low.at[plane, span], strip_s.at[0, number],
                 strip_r.at[0, number], (depth, before)),
            send(strip_high.at[plane, span], got_high.at[plane, span], strip_s.at[1, number],
                 strip_r.at[1, number], (depth, after)),
        ]
        for target, copy, is_high in ((strip_high, pair[1], True), (strip_low, pair[0], False)):
            for start in range(span.start, span.stop, rows // 2):
                at_rows = slice(start, start + rows // 2)
                values = []
                for slot in range(slots):
                    value = came[slot, 0, plane, at_rows]
                    is_low = low[slot, at_rows] > 0.5
                    values.append(
                        jnp.where(is_low, zero, value) if is_high else jnp.where(is_low, value, zero)
                    )
                for at in range(blocks):
                    terms = [
                        jnp.where(blk[slot, : rows // 2] == at, values[slot], zero)
                        for slot in range(slots)
                    ]
                    target[plane, at_rows, columns(at)] = (terms[0] + terms[1]) + (terms[2] + terms[3])
            copy.start()
        strip_copies.append(pair)

    for offset in range(n_depth - 1):
        send(grads.at[0, 1], came.at[0, 1], gb_s.at[offset], gb_r.at[offset],
             (depth, scan)).wait_recv()
    for plane in range(2):
        for piece in range(4):
            at_rows = slice(piece * (rows // 2), (piece + 1) * (rows // 2))
            values = [came[slot, 1, plane, at_rows] for slot in range(slots)]
            for at in range(blocks):
                terms = [
                    jnp.where(blk[slot, : rows // 2] == at, values[slot], zero).astype(F32)
                    for slot in range(slots)
                ]
                total = (terms[0] + terms[1]) + (terms[2] + terms[3])
                out_ref[0, plane, at_rows, columns(at)] = total
    for number, (plane, span) in enumerate(chunks):
        for copy in strip_copies[number]:
            copy.wait_recv()
        out_ref[0, plane, span] = out_ref[0, plane, span] + (
            got_low[plane, span].astype(F32) + got_high[plane, span].astype(F32)
        )

    par_copy.wait_send()
    meas_copy.wait_send()
    for copy in b_copies + a_copies:
        copy.wait_send()
    for pair in tile_copies + strip_copies:
        for copy in pair:
            copy.wait_send()
    for step in range(1, n_depth):
        at = lax.rem(depth + step, n_depth)
        for copy in grad_near(at) + [grad_far(at)]:
            copy.wait_send()


def body(transmission, probe_wave, prop_phase, measured, scan_rows, scan_cols, live_counts):
    width = probe_wave.shape[-1]
    half = transmission.shape[2]
    columns = transmission.shape[3]
    n_depth = lax.axis_size("depth")
    t1, t2 = dft_blocks(width)
    dma = pltpu.SemaphoreType.DMA
    others = n_depth - 1
    scratch = [
        pltpu.SMEM((n_depth,), jnp.int32),
        pltpu.SMEM((n_depth,), jnp.int32),
        pltpu.SMEM((1,), jnp.int32),
        pltpu.VMEM((n_depth, half // 2, width), BF16),
        pltpu.VMEM((n_depth, half, width), BF16),
        pltpu.VMEM((2, half, columns), F32),
        pltpu.VMEM((2, half, columns), BF16),
        pltpu.VMEM((2, width, width), F32),
        pltpu.VMEM((width, width), F32),
        pltpu.VMEM((width, width), F32),
        pltpu.VMEM((width, width), F32),
        pltpu.VMEM((width, width), F32),
        pltpu.VMEM((2, width, width), BF16),
        pltpu.VMEM((2, width, width), BF16),
        pltpu.VMEM((16, width), jnp.int32),
        pltpu.VMEM((16, width), jnp.int32),
        pltpu.VMEM((2, half, columns), BF16),
        pltpu.VMEM((2, half, columns), BF16),
        pltpu.VMEM((others, 2, half, width), BF16),
        pltpu.VMEM((others, 2, half, width), BF16),
        pltpu.VMEM((n_depth, 2, 2, half, width), BF16),
        pltpu.VMEM((2, width, width), F32),
        pltpu.VMEM((n_depth + 1, 2, width, width), BF16),
        pltpu.VMEM((2, width, width), F32),
        pltpu.VMEM((2, width, width), BF16),
        pltpu.VMEM((2, width, width), BF16),
        pltpu.VMEM((n_depth, 2, 2, half, width), BF16),
        pltpu.VMEM((n_depth, 2, 2, half, width), BF16),
        pltpu.VMEM((2, half, columns), BF16),
        pltpu.VMEM((2, half, columns), BF16),
        pltpu.VMEM((2, half, columns), BF16),
        pltpu.VMEM((2, half, columns), BF16),
        dma((10,)),
        dma((2,)),
        dma((2, 4)),
        dma((2, 4)),
        dma((2,)),
        dma((others,)),
        dma((others,)),
        dma((others, 4)),
        dma((others, 4)),
        dma((others,)),
        dma((others,)),
        dma((others, 4)),
        dma((others, 4)),
        dma((2, 4)),
        dma((2, 4)),
    ]
    anywhere = pl.BlockSpec(memory_space=pltpu.HBM)
    return pl.pallas_call(
        kernel,
        out_shape=pltpu.VMEM(transmission.shape, F32),
        in_specs=[anywhere] * 9,
        out_specs=pl.BlockSpec(memory_space=pltpu.VMEM),
        scratch_shapes=scratch,
        compiler_params=pltpu.CompilerParams(
            collective_id=0, has_side_effects=True, vmem_limit_bytes=57_000_000
        ),
    )(transmission, probe_wave, prop_phase, measured, scan_rows, scan_cols, live_counts, t1, t2)


def solution(mesh):
    in_specs = (
        P("depth", None, "scan", None),
        P(),
        P(),
        P("scan", None, None),
        P("scan"),
        P("scan"),
        P("scan"),
    )
    out_specs = P("depth", None, "scan", None)
    return jax.shard_map(body, mesh=mesh, in_specs=in_specs, out_specs=out_specs, check_vma=False)
```
